128 devices in a mesh: tiles: 32 (over z, y, core), members: 4 (over x).
Axes of the slice: x: 4, y: 4, z: 4, core: 2. Of those that a mesh axis runs over, the one named last changes fastest.
Arguments:
- features: bfloat16 [4, 96, 32, 32, 256], P('members', 'tiles'), may hold values from -6 to 6
- conv_one: bfloat16 [3, 3, 256, 256], replicated, may hold values from -0.125 to 0.125
- conv_two: bfloat16 [3, 3, 256, 256], replicated, may hold values from -0.125 to 0.125
- cotangent: bfloat16 [4, 96, 32, 32, 256], P('members', 'tiles'), may hold values from -6 to 6
- neighbour_tile: int32 [96, 4], P('tiles'), may hold values from 0 to 95, as said below
- rotation: int32 [96, 4], P('tiles'), may hold values from 0 to 7
Outputs:
- output: bfloat16 [4, 96, 32, 32, 256], P('members', 'tiles')
- grad_features: bfloat16 [4, 96, 32, 32, 256], P('members', 'tiles')
- grad_one: float32 [3, 3, 256, 256], replicated
- grad_two: float32 [3, 3, 256, 256], replicated
The draws below stay inside these ranges and needn't reach their ends.
Inputs may be any that keep to these rules, and one draw needn't show every extreme that they name: neighbour_tile and rotation describe the tiles of the six faces of a cube, 16 of them on each face in a square: each tile edge borders exactly one edge of another tile, and the relation is symmetric: if t2 = neighbour_tile[t, e] and e2 = rotation[t, e] % 4 then neighbour_tile[t2, e2] = t and rotation[t2, e2] = e + 4 * (rotation[t, e] // 4).
All inputs are finite; a program needn't handle non-finite values.
Results may differ from the reference program's by a relative error of at most 0.0051.
Values may be sent and summed in bfloat16 or wider, within the bound.
A program may use at most 128 MiB of HBM per device.

```python
import math
import jax
import jax.numpy as jnp
import numpy as np
from jax import lax

CH = 256
TS = 32
TILES = 96
MEMBERS = 4


face_frames = np.array([[[1, 0, 0], [0, 1, 0], [0, 0, 1]], [[-1, 0, 0], [0, 0, 1], [0, 1, 0]], [[0, 1, 0], [0, 0, 1], [1, 0, 0]], [[0, -1, 0], [1, 0, 0], [0, 0, 1]], [[0, 0, 1], [1, 0, 0], [0, 1, 0]], [[0, 0, -1], [0, 1, 0], [1, 0, 0]]], dtype=np.int32)


def cube_links(key):
    side = math.isqrt(TILES // 6)
    tiles_all = 6 * side * side
    index = np.arange(tiles_all)
    face_id = index // (side * side)
    a_pos = index // side % side
    b_pos = index % side
    normal = face_frames[face_id, 0]
    axis_u = face_frames[face_id, 1]
    axis_v = face_frames[face_id, 2]
    width = 2 * side + 1
    base = jax.random.fold_in(key, 811)
    turns = jax.random.randint(jax.random.fold_in(base, 1), (tiles_all,), 0, 8)
    labels = jax.random.permutation(jax.random.fold_in(base, 2), tiles_all).astype(jnp.int32)
    swap_bit = turns % 2
    flip_r = turns // 2 % 2
    flip_s = turns // 4
    corners = []
    for r_loc in (0, 1):
        for s_loc in (0, 1):
            r_turn = (r_loc + flip_r) % 2
            s_turn = (s_loc + flip_s) % 2
            off_a = jnp.where(swap_bit == 1, s_turn, r_turn)
            off_b = jnp.where(swap_bit == 1, r_turn, s_turn)
            point = side * normal + (2 * (a_pos + off_a) - side)[:, None] * axis_u + (2 * (b_pos + off_b) - side)[:, None] * axis_v
            code = (point[:, 0] + side) * width * width + (point[:, 1] + side) * width + (point[:, 2] + side)
            corners.append(code.astype(jnp.int32))
    start_pt = jnp.stack([corners[0], corners[2], corners[0], corners[1]], axis=1).reshape(-1)
    end_pt = jnp.stack([corners[1], corners[3], corners[2], corners[3]], axis=1).reshape(-1)
    edges_all = 4 * tiles_all
    iota_e = jnp.arange(edges_all, dtype=jnp.int32)
    forward = (start_pt[:, None] == start_pt[None, :]) & (end_pt[:, None] == end_pt[None, :])
    backward = (start_pt[:, None] == end_pt[None, :]) & (end_pt[:, None] == start_pt[None, :])
    matched = (forward | backward) & (iota_e[:, None] != iota_e[None, :])
    partner = jnp.sum(matched.astype(jnp.int32) * iota_e[None, :], axis=1)
    reversed_flag = (start_pt[partner] != start_pt).astype(jnp.int32)
    partner_tile = (partner // 4).reshape(tiles_all, 4)
    partner_edge = (partner % 4).reshape(tiles_all, 4)
    reversed_flag = reversed_flag.reshape(tiles_all, 4)
    neighbours = jnp.zeros((tiles_all, 4), jnp.int32).at[labels].set(labels[partner_tile])
    codes = jnp.zeros((tiles_all, 4), jnp.int32).at[labels].set(partner_edge + 4 * reversed_flag)
    return (neighbours, codes)


def draw_neighbour_tile(key, part):
    return cube_links(key)[0]


def draw_rotation(key, part):
    return cube_links(key)[1]


def level_of(key, extent, pieces, smallest, top_value):
    factor_of, own = 1.0, jax.random.fold_in(key, 6)
    for position, blocks in pieces:
        draws = jnp.exp(jax.random.uniform(jax.random.fold_in(own, position), (blocks,), jnp.float32, smallest / len(pieces), top_value / len(pieces)))
        factor_of = factor_of * jnp.repeat(draws, extent[position] // blocks).reshape([-1 if axis == position else 1 for axis in range(len(extent))])
    return factor_of


def bell_draw(rng, dims, scale, limit, cuts=(), held_as=jnp.bfloat16):
    entries = scale * jax.random.normal(rng, dims, jnp.float32)
    if cuts:
        entries = entries * level_of(rng, dims, cuts, -0.22, 0.18)
    return jnp.clip(entries, -limit, limit).astype(held_as)


def setup_inputs(seed: int = 0) -> dict:
    splits = jax.random.split(jax.random.key(seed), 7)
    return {
        "features": bell_draw(splits[0], (MEMBERS, TILES, TS, TS, CH), 1.0, 6.0, ((0, 4), (1, 32))),
        "conv_one": bell_draw(splits[1], (3, 3, CH, CH), (9 * CH) ** -0.5, 0.125),
        "conv_two": bell_draw(splits[2], (3, 3, CH, CH), (9 * CH) ** -0.5, 0.125),
        "cotangent": bell_draw(splits[3], (MEMBERS, TILES, TS, TS, CH), 1.0, 6.0, ((0, 4), (1, 32))),
        "neighbour_tile": draw_neighbour_tile(jax.random.fold_in(splits[6], 71), 0),
        "rotation": draw_rotation(jax.random.fold_in(splits[6], 71), 0),
    }


def edges_of(values):
    top_edge = values[:, 0]
    bottom_edge = values[:, -1]
    left_edge = values[:, :, 0]
    right_edge = values[:, :, -1]
    stacked = jnp.stack([top_edge, bottom_edge, left_edge, right_edge], axis=1)
    return stacked.reshape(-1, values.shape[2], values.shape[3])

def orient(seam_vals, rotation):
    flipped = (rotation // 4)[:, :, None, None] == 1
    return jnp.where(flipped, seam_vals[:, :, ::-1], seam_vals)

def seam_rows(edge_list, neighbour_tile, rotation):
    source = (4 * neighbour_tile + rotation % 4).astype(jnp.int32)
    return orient(edge_list[source], rotation)

def pad_tiles(values, seam_vals):
    zero_col = jnp.zeros_like(seam_vals[:, 0, :1])
    top_row = jnp.concatenate([zero_col, seam_vals[:, 0], zero_col], axis=1)[:, None]
    bottom_row = jnp.concatenate([zero_col, seam_vals[:, 1], zero_col], axis=1)[:, None]
    middle = jnp.concatenate([seam_vals[:, 2][:, :, None], values, seam_vals[:, 3][:, :, None]], axis=2)
    return jnp.concatenate([top_row, middle, bottom_row], axis=1)

def outer_rows(padded):
    return jnp.stack([padded[:, 0, 1:-1], padded[:, -1, 1:-1], padded[:, 1:-1, 0], padded[:, 1:-1, -1]], axis=1)

def add_edges(interior, returned):
    interior = interior.at[:, 0].add(returned[:, 0])
    interior = interior.at[:, -1].add(returned[:, 1])
    interior = interior.at[:, :, 0].add(returned[:, 2])
    return interior.at[:, :, -1].add(returned[:, 3])

def matmul(left, right):
    return jnp.dot(left, right, precision=lax.Precision.HIGHEST, preferred_element_type=jnp.float32)

def convolve(padded, kernel):
    tiles_n = padded.shape[0]
    side = padded.shape[1] - 2
    chans = padded.shape[3]
    total = jnp.zeros((tiles_n * side * side, kernel.shape[3]), jnp.float32)
    for row_a in range(3):
        for col_b in range(3):
            window = padded[:, row_a:row_a + side, col_b:col_b + side].reshape(-1, chans)
            total = total + matmul(window, kernel[row_a, col_b])
    return total.reshape(tiles_n, side, side, kernel.shape[3])

def spread(gradient, kernel):
    tiles_n = gradient.shape[0]
    side = gradient.shape[1]
    chans = gradient.shape[3]
    wide = side + 2
    framed = jnp.pad(gradient, ((0, 0), (2, 2), (2, 2), (0, 0)))
    total = jnp.zeros((tiles_n * wide * wide, kernel.shape[2]), jnp.float32)
    for row_a in range(3):
        for col_b in range(3):
            window = framed[:, 2 - row_a:2 - row_a + wide, 2 - col_b:2 - col_b + wide].reshape(-1, chans)
            total = total + matmul(window, kernel[row_a, col_b].T)
    return total.reshape(tiles_n, wide, wide, kernel.shape[2])

def kernel_grad(padded, gradient):
    side = gradient.shape[1]
    chans = padded.shape[3]
    flat_grad = gradient.reshape(-1, gradient.shape[3])
    taps = []
    for row_a in range(3):
        for col_b in range(3):
            window = padded[:, row_a:row_a + side, col_b:col_b + side].reshape(-1, chans)
            taps.append(matmul(window.T, flat_grad))
    return jnp.stack(taps, axis=0).reshape(3, 3, chans, gradient.shape[3])

def return_rims(spread_out, neighbour_tile, rotation):
    interior = spread_out[:, 1:-1, 1:-1]
    rim_vals = outer_rows(spread_out).astype(jnp.bfloat16)
    rim_list = rim_vals.reshape(-1, rim_vals.shape[2], rim_vals.shape[3])
    returned = seam_rows(rim_list, neighbour_tile, rotation).astype(jnp.float32)
    return add_edges(interior, returned)

def reference(features, conv_one, conv_two, cotangent, neighbour_tile, rotation):
    kernel_one = conv_one.astype(jnp.float32)
    kernel_two = conv_two.astype(jnp.float32)

    def member(inputs):
        values, grad_out = inputs
        padded_in = pad_tiles(values, seam_rows(edges_of(values), neighbour_tile, rotation))
        padded_in32 = padded_in.astype(jnp.float32)
        preact = convolve(padded_in32, kernel_one)
        activation = jax.nn.silu(preact).astype(jnp.bfloat16)
        padded_act = pad_tiles(activation, seam_rows(edges_of(activation), neighbour_tile, rotation))
        padded_act32 = padded_act.astype(jnp.float32)
        result = convolve(padded_act32, kernel_two).astype(jnp.bfloat16)
        grad_out32 = grad_out.astype(jnp.float32)
        second = kernel_grad(padded_act32, grad_out32)
        d_act = return_rims(spread(grad_out32, kernel_two), neighbour_tile, rotation)
        sigmoid_v = jax.nn.sigmoid(preact)
        d_pre = (d_act * sigmoid_v * (1.0 + preact * (1.0 - sigmoid_v))).astype(jnp.bfloat16)
        d_pre32 = d_pre.astype(jnp.float32)
        first = kernel_grad(padded_in32, d_pre32)
        grad_in = return_rims(spread(d_pre32, kernel_one), neighbour_tile, rotation).astype(jnp.bfloat16)
        return (result, grad_in, first, second)
    output, grad_features, firsts, seconds = lax.map(member, (features, cotangent))
    factor = 1.0 / math.sqrt(MEMBERS * TILES * TS * TS)
    grad_one = lax.optimization_barrier(jnp.sum(firsts, axis=0)) * factor
    grad_two = lax.optimization_barrier(jnp.sum(seconds, axis=0)) * factor
    return (output, grad_features, grad_one, grad_two)
```

```python
import functools
import math

import jax
import jax.numpy as jnp
from jax import lax
from jax.experimental import pallas as pl
from jax.experimental.pallas import tpu as pltpu
from jax.sharding import PartitionSpec as P

MESH = pl.DeviceIdType.MESH
F32 = jnp.float32
BF16 = jnp.bfloat16
ROWS = 512


def kernel(
    feat, cot, w1, w2, tab, loc,
    out, gfeat, full1, full2,
    fa3, c3, d3, wt, pre, dact, xt, grad, seams, edges, mats,
    edge_out, ag0, ag1, ag2, ag3, pick, got0, got1, got2, got3, tabv, tabs,
    corr, snd, rcore, sx, rx, sy, ry, sz, rz,
    tab_s, tab_r, ag_s, ag_r, pk_s, pk_r, ar_s, ar_r, loc_sem,
):
    ag = (ag0, ag1, ag2, ag3)
    got = (got0, got1, got2, got3)
    me = lax.axis_index("tiles")
    xpos = lax.axis_index("members")
    core = lax.rem(me, 2)
    ypos = lax.rem(me // 2, 4)
    zpos = me // 8
    ring = zpos * (1 - core) + ypos * core
    other = ypos * (1 - core) + zpos * core

    def tid(z, y, c):
        return (z * 4 + y) * 2 + c

    partner = tid(zpos, ypos, 1 - core)

    def wrap(v):
        return lax.rem(v, 4)

    barrier = pltpu.get_barrier_semaphore()
    pl.semaphore_signal(barrier, inc=1, device_id={"tiles": partner}, device_id_type=MESH)
    for d in range(1, 4):
        for c in range(2):
            pl.semaphore_signal(barrier, inc=1, device_id={"tiles": tid(wrap(zpos + d), ypos, c)}, device_id_type=MESH)
            pl.semaphore_signal(barrier, inc=1, device_id={"tiles": tid(zpos, wrap(ypos + d), c)}, device_id_type=MESH)
        pl.semaphore_signal(barrier, inc=1, device_id={"members": wrap(xpos + d)}, device_id_type=MESH)
    pl.semaphore_wait(barrier, 16)

    def remote(src, dst, ssem, rsem, target):
        return pltpu.make_async_remote_copy(
            src_ref=src, dst_ref=dst, send_sem=ssem, recv_sem=rsem,
            device_id={"tiles": target}, device_id_type=MESH,
        )

    def remote_x(src, dst, ssem, rsem, target):
        return pltpu.make_async_remote_copy(
            src_ref=src, dst_ref=dst, send_sem=ssem, recv_sem=rsem,
            device_id={"members": target}, device_id_type=MESH,
        )

    tab_copies = []
    for d in range(1, 4):
        tab_copies.append(remote(tab.at[0], tabv.at[ypos * 2 + core], tab_s.at[d - 1], tab_r.at[ypos * 2 + core], tid(zpos, wrap(ypos + d), 0)))
        tab_copies.append(remote(tab.at[1], tabv.at[zpos * 2 + core], tab_s.at[d + 2], tab_r.at[zpos * 2 + core], tid(wrap(zpos + d), ypos, 1)))
    slot_p = (ypos * core + zpos * (1 - core)) * 2 + core
    tab_copies.append(remote(tab.at[1 - core], tabv.at[slot_p], tab_s.at[6], tab_r.at[slot_p], partner))
    for copy in tab_copies:
        copy.start()
    tab_own = pltpu.make_async_copy(tab.at[core], tabv.at[other * 2 + core], loc_sem.at[0])
    tab_own.start()

    r_i = lax.broadcasted_iota(jnp.int32, (128, 1024), 0)
    c_i = lax.broadcasted_iota(jnp.int32, (128, 1024), 1)
    e_i = r_i // 32
    k_i = r_i - e_i * 32
    want = jnp.where(e_i == 0, k_i, jnp.where(e_i == 1, 992 + k_i, jnp.where(e_i == 2, 32 * k_i, 32 * k_i + 31)))
    pickrow = jnp.where(c_i == want, 1.0, 0.0).astype(BF16)
    m_r = lax.broadcasted_iota(jnp.int32, (96, 32), 0)
    m_c = lax.broadcasted_iota(jnp.int32, (96, 32), 1)
    m_b = m_r // 32
    m_t = m_r - m_b * 32 + m_b - 1
    mats[0] = jnp.where(m_c == m_t, 1.0, 0.0).astype(BF16)
    mats[1] = jnp.where((31 - m_c == m_t), 1.0, 0.0).astype(BF16)

    def dot(a, b):
        return jnp.dot(a, b, preferred_element_type=F32)

    def dot_nt(a, b):
        return lax.dot_general(a, b, (((1,), (1,)), ((), ())), preferred_element_type=F32)

    def dot_tn(a, b):
        return lax.dot_general(a, b, (((0,), (0,)), ((), ())), preferred_element_type=F32)

    def take_edges(get, which):
        for t in range(3):
            picked = dot(pickrow, get(t)).astype(BF16)
            for e in range(4):
                edges[which, e, t * 32:t * 32 + 32, :] = picked[e * 32:e * 32 + 32]

    def put_edge(n, t, e, value):
        edge_out[n, 0, t * 4 + e] = value[:, 0:128]
        edge_out[n, 1, t * 4 + e] = value[:, 128:256]

    def send_edges(n):
        copies = []
        for d in range(1, 4):
            copies.append(remote(edge_out.at[n, 0], ag[n].at[pl.ds((zpos * 2 + core) * 12, 12)], ag_s.at[n, d - 1], ag_r.at[n, zpos * 2 + core], tid(wrap(zpos + d), ypos, 0)))
            copies.append(remote(edge_out.at[n, 1], ag[n].at[pl.ds((ypos * 2 + core) * 12, 12)], ag_s.at[n, d + 2], ag_r.at[n, ypos * 2 + core], tid(zpos, wrap(ypos + d), 1)))
        slot = (zpos * core + ypos * (1 - core)) * 2 + core
        copies.append(remote(edge_out.at[n, 1 - core], ag[n].at[pl.ds((slot) * 12, 12)], ag_s.at[n, 6], ag_r.at[n, slot], partner))
        for copy in copies:
            copy.start()
        own = pltpu.make_async_copy(edge_out.at[n, core], ag[n].at[pl.ds((ring * 2 + core) * 12, 12)], loc_sem.at[1])
        own.start()
        own.wait()
        return copies

    def forward(n):
        for d in range(1, 4):
            for c in range(2):
                slot = wrap(ring + d) * 2 + c
                remote(edge_out.at[n, 0], ag[n].at[pl.ds((slot) * 12, 12)], ag_s.at[n, 0], ag_r.at[n, slot], partner).wait_recv()
        slot = ring * 2 + 1 - core
        remote(edge_out.at[n, 0], ag[n].at[pl.ds((slot) * 12, 12)], ag_s.at[n, 0], ag_r.at[n, slot], partner).wait_recv()

        def choose(q, carry):
            for k in range(12):
                pick[n, q, k] = ag[n][tabs[q, 0, k]]
            return carry

        lax.fori_loop(0, 8, choose, 0)
        copies = []
        for d in range(1, 4):
            p = wrap(other + d)
            for c in range(2):
                target = tid(zpos * (1 - core) + p * core, p * (1 - core) + ypos * core, c)
                copies.append(remote(pick.at[n, p * 2 + c], got[n].at[core, other], pk_s.at[n, d * 2 + c - 2], pk_r.at[n, core * 4 + other], target))
        copies.append(remote(pick.at[n, other * 2 + 1 - core], got[n].at[core, other], pk_s.at[n, 6], pk_r.at[n, core * 4 + other], partner))
        for copy in copies:
            copy.start()
        own = pltpu.make_async_copy(pick.at[n, other * 2 + core], got[n].at[core, other], loc_sem.at[2])
        own.start()
        own.wait()
        return copies

    def arrive(n):
        def wait(h, p):
            remote(pick.at[n, 0], got[n].at[h, p], pk_s.at[n, 0], pk_r.at[n, h * 4 + p], partner).wait_recv()

        for d in range(1, 4):
            wait(0, wrap(ypos + d))
            wait(1, wrap(zpos + d))
        wait(1 - core, zpos * (1 - core) + ypos * core)

    def received(n, k):
        left = got[n][0, loc[0, k], k]
        right = got[n][1, loc[1, k], k]
        return jnp.concatenate([left, right], axis=1)

    def take_seams(n):
        for t in range(3):
            for e in range(4):
                k = t * 4 + e
                both = dot(mats[loc[2, k]], received(n, k)).astype(BF16)
                for b in range(3):
                    seams[e, t * 32:t * 32 + 32, b * 256:b * 256 + 256] = both[b * 32:b * 32 + 32]

    jj = lax.rem(lax.broadcasted_iota(jnp.int32, (128, 256), 0), 32)

    def put3(dst, t, r, x):
        row = pl.multiple_of(32 + r * 128, 32)
        dst[t, pl.ds(row, 128), 256:512] = x.astype(BF16)
        dst[t, pl.ds(row, 128), 0:256] = jnp.where(jj == 0, 0.0, pltpu.roll(x, 1, 0)).astype(BF16)
        dst[t, pl.ds(row, 128), 512:768] = jnp.where(jj == 31, 0.0, pltpu.roll(x, 127, 0)).astype(BF16)

    def each_chunk(body):
        def step(i, carry):
            t = i // 8
            body(t, i - t * 8)
            return carry

        lax.fori_loop(0, 24, step, 0)

    def conv3(x3, weight, store):
        parts = 1024 // ROWS

        def step(i, carry):
            t = i // parts
            r = (i - t * parts) * ROWS
            acc = dot(x3[t, pl.ds(pl.multiple_of(r, 32), ROWS), :], weight(0))
            acc = acc + dot(x3[t, pl.ds(pl.multiple_of(r + 32, 32), ROWS), :], weight(1))
            acc = acc + dot(x3[t, pl.ds(pl.multiple_of(r + 64, 32), ROWS), :], weight(2))
            store(t, pl.multiple_of(r, 128), acc)
            return carry

        lax.fori_loop(0, 3 * parts, step, 0)

    def edge_weight(w, e):
        return [w[0, 0], w[0, 1], w[0, 2]] if e == 0 else [w[2, 0], w[2, 1], w[2, 2]] if e == 1 else [w[0, 0], w[1, 0], w[2, 0]] if e == 2 else [w[0, 2], w[1, 2], w[2, 2]]

    eight = lax.broadcasted_iota(jnp.int32, (8, 256), 0)

    def add_edge(dst, t, e, value_of):
        if e < 2:
            row = 0 if e == 0 else 992
            dst[t, row:row + 32, :] += value_of[t * 32:t * 32 + 32, :]
        else:
            base = 0 if e == 2 else 24
            at = 0 if e == 2 else 7

            def step(i, carry):
                row = pl.multiple_of(i * 32 + base, 8)
                line = value_of[pl.ds(t * 32 + i, 1), :]
                dst[t, pl.ds(row, 8), :] += jnp.where(eight == at, jnp.broadcast_to(line, (8, 256)), 0.0)
                return carry

            lax.fori_loop(0, 32, step, 0)

    def seam_conv(w, dst, corr):
        for e in range(4):
            ws = edge_weight(w, e)
            corr[...] = dot(seams[e, :, 0:256], ws[0]) + dot(seams[e, :, 256:512], ws[1]) + dot(seams[e, :, 512:768], ws[2])
            for t in range(3):
                add_edge(dst, t, e, corr)

    def rim_add(n, dst, corr):
        for e in range(4):
            for t in range(3):
                k = t * 4 + e
                corr[t * 32:t * 32 + 32, :] = dot(mats[loc[2, k], 32:64, :], received(n, k))
            for t in range(3):
                add_edge(dst, t, e, corr)

    def rims(which, w, n):
        for e in range(4):
            ws = edge_weight(w, e)
            for t in range(3):
                row = edges[which, e, t * 32:t * 32 + 32, :]
                three = dot(mats[0], row).astype(BF16)
                value = dot_nt(three[64:96], ws[0]) + dot_nt(three[32:64], ws[1]) + dot_nt(three[0:32], ws[2])
                put_edge(n, t, e, value.astype(BF16))

    def transpose_tile(x3, t):
        eye = jnp.where(lax.broadcasted_iota(jnp.int32, (256, 256), 0) == lax.broadcasted_iota(jnp.int32, (256, 256), 1), 1.0, 0.0).astype(BF16)
        xt[t] = dot_nt(eye, x3[t, 32:1056, 256:512]).astype(BF16)

    def turn_weight(w):
        for a in range(3):
            for b in range(3):
                wt[a, b * 256:b * 256 + 256, :] = w[2 - a, 2 - b].T

    def put_grad(a, b, value, first):
        for h in range(2):
            block = value[:, h * 128:h * 128 + 128].reshape(4, 4, 16, 128)
            if first:
                grad[h, :, :, a * 3 + b] = block
            else:
                grad[h, :, :, a * 3 + b] += block

    def grad_inner(g3):
        for t in range(3):
            for al in range(3):
                def step(be, carry):
                    value = dot(xt[t], g3[t, al * 32:al * 32 + 1024, pl.ds(pl.multiple_of(be * 256, 256), 256)])
                    ab = (2 - al) * 3 + 2 - be
                    for h in range(2):
                        block = value[:, h * 128:h * 128 + 128].reshape(4, 4, 16, 128)
                        if t == 0:
                            grad[h, :, :, ab] = block
                        else:
                            grad[h, :, :, ab] += block
                    return carry

                lax.fori_loop(0, 3, step, 0)

    def grad_seams(which):
        for e in range(4):
            for b in range(3):
                value = dot_tn(seams[e, :, b * 256:b * 256 + 256], edges[which, e])
                a, bb = [(0, b), (2, b), (b, 0), (b, 2)][e]
                put_grad(a, bb, value, False)

    def reduce_start(g):
        def step(i, carry):
            h = i // 4
            v = i - h * 4
            snd[g, h, v] = grad[h, v].astype(BF16)
            return carry

        lax.fori_loop(0, 8, step, 0)
        copy = remote(snd.at[g, 1 - core], rcore.at[g], ar_s.at[g, 0], ar_r.at[g, 0], partner)
        copy.start()
        return copy

    def reduce_finish(g, first, full):
        first.wait_recv()

        def add_core(i, carry):
            sx[g, i] = (grad[core, i] + rcore[g, i].astype(F32)).astype(BF16)
            return carry

        lax.fori_loop(0, 4, add_core, 0)
        sends = [first]

        def swap(src_of, dst_of, base, mine, send, target_of):
            cs = []
            for d in range(1, 4):
                p = wrap(mine + d)
                cs.append(send(src_of(p), dst_of(mine), ar_s.at[g, base + d - 1], ar_r.at[g, base + mine], target_of(p)))
            for c in cs:
                c.start()
            for d in range(1, 4):
                p = wrap(mine + d)
                send(src_of(p), dst_of(p), ar_s.at[g, base], ar_r.at[g, base + p], target_of(p)).wait_recv()
            sends.extend(cs)

        to_x = lambda p: p
        to_y = lambda p: tid(zpos, p, core)
        to_z = lambda p: tid(p, ypos, core)
        swap(lambda p: sx.at[g, p], lambda p: rx.at[g, p], 1, xpos, remote_x, to_x)
        total = sx[g, xpos].astype(F32)
        for d in range(1, 4):
            total = total + rx[g, wrap(xpos + d)].astype(F32)
        sy[g] = total.astype(BF16)
        swap(lambda p: sy.at[g, p], lambda p: ry.at[g, p], 5, ypos, remote, to_y)
        total = sy[g, ypos].astype(F32)
        for d in range(1, 4):
            total = total + ry[g, wrap(ypos + d)].astype(F32)
        sz[g] = total.astype(BF16)
        swap(lambda p: sz.at[g], lambda p: rz.at[g, p], 9, zpos, remote, to_z)
        rz[g, zpos] = sz[g]
        total = rz[g, 0].astype(F32) + rz[g, 1].astype(F32) + rz[g, 2].astype(F32) + rz[g, 3].astype(F32)
        full[core, xpos, ypos] = total.astype(BF16)
        swap(lambda p: full.at[core, xpos, ypos], lambda p: full.at[core, xpos, p], 13, ypos, remote, to_y)
        swap(lambda p: full.at[core, xpos], lambda p: full.at[core, p], 17, xpos, remote_x, to_x)
        last = remote(full.at[core], full.at[core], ar_s.at[g, 21], ar_r.at[g, 21], partner)
        last.start()
        remote(full.at[1 - core], full.at[1 - core], ar_s.at[g, 21], ar_r.at[g, 21], partner).wait_recv()
        sends.append(last)
        return sends

    sends = []
    take_edges(lambda t: feat[t].reshape(1024, 256), 0)
    for t in range(3):
        for e in range(4):
            put_edge(0, t, e, edges[0, e, t * 32:t * 32 + 32, :])
    sends += send_edges(0)
    take_edges(lambda t: cot[t].reshape(1024, 256), 1)
    rims(1, w2, 1)
    sends += send_edges(1)

    for x3 in (fa3, c3, d3):
        x3[:, 0:32, :] = jnp.zeros((3, 32, 768), BF16)
        x3[:, 1056:1088, :] = jnp.zeros((3, 32, 768), BF16)

    def load_feat(t, r):
        put3(fa3, t, r, feat[t, pl.ds(r * 4, 4)].reshape(128, 256).astype(F32))

    def load_cot(t, r):
        put3(c3, t, r, cot[t, pl.ds(r * 4, 4)].reshape(128, 256).astype(F32))

    each_chunk(load_feat)
    for d in range(1, 4):
        for c in range(2):
            slot = wrap(other + d) * 2 + c
            remote(tab.at[0], tabv.at[slot], tab_s.at[0], tab_r.at[slot], partner).wait_recv()
    slot = other * 2 + 1 - core
    remote(tab.at[0], tabv.at[slot], tab_s.at[0], tab_r.at[slot], partner).wait_recv()
    tab_own.wait()
    to_smem = pltpu.make_async_copy(tabv, tabs, loc_sem.at[3])
    to_smem.start()
    to_smem.wait()

    def store_pre(t, r, acc):
        pre[t, pl.ds(r, ROWS), :] = acc

    def store_dact(t, r, acc):
        dact[t, pl.ds(r, ROWS), :] = acc

    conv3(fa3, lambda a: w1[a].reshape(768, 256), store_pre)
    sends += forward(0)
    each_chunk(load_cot)
    turn_weight(w2)
    conv3(c3, lambda a: wt[a], store_dact)
    sends += forward(1)
    for t in range(3):
        transpose_tile(fa3, t)
    turn_weight(w1)

    arrive(0)
    take_seams(0)
    seam_conv(w1, pre, corr)
    arrive(1)
    rim_add(1, dact, corr)

    def nonlinear(t, r):
        row = pl.multiple_of(r * 128, 128)
        u = pre[t, pl.ds(row, 128), :]
        s = 1.0 / (1.0 + jnp.exp(-u))
        put3(fa3, t, r, (u * s).astype(BF16).astype(F32))
        d = dact[t, pl.ds(row, 128), :] * s * (1.0 + u * (1.0 - s))
        put3(d3, t, r, d.astype(BF16).astype(F32))

    each_chunk(nonlinear)

    take_edges(lambda t: fa3[t, 32:1056, 256:512], 2)
    for t in range(3):
        for e in range(4):
            put_edge(2, t, e, edges[2, e, t * 32:t * 32 + 32, :])
    sends += send_edges(2)
    take_edges(lambda t: d3[t, 32:1056, 256:512], 0)
    rims(0, w1, 3)
    sends += send_edges(3)
    grad_inner(d3)
    grad_seams(0)
    first1 = reduce_start(0)
    sends += forward(2)
    sends += reduce_finish(0, first1, full1)
    for t in range(3):
        transpose_tile(fa3, t)
    conv3(fa3, lambda a: w2[a].reshape(768, 256), store_pre)
    sends += forward(3)
    conv3(d3, lambda a: wt[a], store_dact)
    grad_inner(c3)
    arrive(2)
    take_seams(2)
    grad_seams(1)
    first2 = reduce_start(1)
    seam_conv(w2, pre, corr)
    arrive(3)
    rim_add(3, dact, corr)

    def finish(t, r):
        row = pl.multiple_of(r * 128, 128)
        out[t, pl.ds(row, 128), :] = pre[t, pl.ds(row, 128), :].astype(BF16)
        gfeat[t, pl.ds(row, 128), :] = dact[t, pl.ds(row, 128), :].astype(BF16)

    each_chunk(finish)
    sends += reduce_finish(1, first2, full2)
    for copy in sends + tab_copies:
        copy.wait_send()


def on_device(features, conv_one, conv_two, cotangent, neighbour_tile, rotation):
    cells_all = lax.axis_size("members") * lax.axis_size("tiles") * 3 * 1024
    factor = 1.0 / math.sqrt(cells_all)
    source = (4 * neighbour_tile + rotation % 4).reshape(12)
    device = source // 12
    z_of, y_of, c_of, row = device // 8, device // 2 % 4, device % 2, source % 12
    tab = jnp.stack([(z_of * 2 + c_of) * 12 + row, (y_of * 2 + c_of) * 12 + row])
    tab = jnp.broadcast_to(jnp.pad(tab, ((0, 0), (0, 116)))[:, None], (2, 8, 128))
    loc = jnp.stack([y_of, z_of, (rotation // 4).reshape(12)])
    vmem = pl.BlockSpec(memory_space=pltpu.VMEM)
    dma = pltpu.SemaphoreType.DMA
    out, gfeat, full1, full2 = pl.pallas_call(
        kernel,
        out_shape=(
            jax.ShapeDtypeStruct((3, 1024, 256), BF16),
            jax.ShapeDtypeStruct((3, 1024, 256), BF16),
            jax.ShapeDtypeStruct((2, 4, 4, 9, 16, 128), BF16),
            jax.ShapeDtypeStruct((2, 4, 4, 9, 16, 128), BF16),
        ),
        in_specs=[vmem] * 5 + [pl.BlockSpec(memory_space=pltpu.SMEM)],
        out_specs=(vmem,) * 4,
        scratch_shapes=[
            pltpu.VMEM((3, 1088, 768), BF16),
            pltpu.VMEM((3, 1088, 768), BF16),
            pltpu.VMEM((3, 1088, 768), BF16),
            pltpu.VMEM((3, 768, 256), BF16),
            pltpu.VMEM((3, 1024, 256), F32),
            pltpu.VMEM((3, 1024, 256), F32),
            pltpu.VMEM((3, 256, 1024), BF16),
            pltpu.VMEM((2, 4, 4, 9, 16, 128), F32),
            pltpu.VMEM((4, 96, 768), BF16),
            pltpu.VMEM((3, 4, 96, 256), BF16),
            pltpu.VMEM((2, 96, 32), BF16),
            pltpu.VMEM((4, 2, 12, 32, 128), BF16),
            *[pltpu.VMEM((96, 32, 128), BF16)] * 4,
            pltpu.VMEM((4, 8, 12, 32, 128), BF16),
            *[pltpu.VMEM((2, 4, 12, 32, 128), BF16)] * 4,
            pltpu.VMEM((8, 8, 128), jnp.int32),
            pltpu.SMEM((8, 8, 128), jnp.int32),
            pltpu.VMEM((96, 256), F32),
            pltpu.VMEM((2, 2, 4, 4, 9, 16, 128), BF16),
            pltpu.VMEM((2, 4, 4, 9, 16, 128), BF16),
            pltpu.VMEM((2, 4, 4, 9, 16, 128), BF16),
            pltpu.VMEM((2, 4, 4, 9, 16, 128), BF16),
            pltpu.VMEM((2, 4, 9, 16, 128), BF16),
            pltpu.VMEM((2, 4, 9, 16, 128), BF16),
            pltpu.VMEM((2, 9, 16, 128), BF16),
            pltpu.VMEM((2, 4, 9, 16, 128), BF16),
            dma((7,)),
            dma((8,)),
            dma((4, 7)),
            dma((4, 8)),
            dma((4, 7)),
            dma((4, 8)),
            dma((2, 22)),
            dma((2, 22)),
            dma((4,)),
        ],
        compiler_params=pltpu.CompilerParams(
            collective_id=0, has_side_effects=True, vmem_limit_bytes=67043328
        ),
    )(features[0], cotangent[0], conv_one, conv_two, tab, loc)

    def whole(full):
        return jnp.transpose(full.astype(F32) * factor, (3, 1, 2, 4, 0, 5)).reshape(3, 3, 256, 256)

    shape = features.shape
    return (out.reshape(shape), gfeat.reshape(shape), whole(full1), whole(full2))


def solution(mesh):
    placed = (
        P("members", "tiles", None, None, None),
        P(),
        P(),
        P("members", "tiles", None, None, None),
        P("tiles", None),
        P("tiles", None),
    )
    return jax.shard_map(
        on_device,
        mesh=mesh,
        in_specs=placed,
        out_specs=(
            P("members", "tiles", None, None, None),
            P("members", "tiles", None, None, None),
            P(),
            P(),
        ),
        check_vma=False,
    )
```

```python
import functools
import math

import jax
import jax.numpy as jnp
from jax import lax
from jax.experimental import pallas as pl
from jax.experimental.pallas import tpu as pltpu
from jax.sharding import PartitionSpec as P

MESH = pl.DeviceIdType.MESH
F32 = jnp.float32
BF16 = jnp.bfloat16
ROWS = 512


ORDER = ("xyz", "yzx", "zxy")


def kernel(
    feat_hbm, cot_hbm, w1_hbm, w2_hbm, tab, loc,
    out, gfeat, gout1, gout2,
    feat, cot, w1, w2,
    fa3, c3, d3, wt, pre, dact, xt, grad1, grad2, seams, edges, rimrows, corr, mats, pickrow,
    edge_out, ag0, ag1, ag2, ag3, pick, got0, got1, got2, got3, tabv, tabs,
    snd, rcore, sx, rx, sy, ry, sz, rz, full,
    tab_s, tab_r, ag_s, ag_r, pk_s, pk_r, ar_s, ar_r, loc_sem, in_sem,
):
    ag = (ag0, ag1, ag2, ag3)
    got = (got0, got1, got2, got3)
    grads = (grad1, grad2)
    gouts = (gout1, gout2)
    loads = [
        pltpu.make_async_copy(src, dst, in_sem.at[i])
        for i, (src, dst) in enumerate(((feat_hbm, feat), (cot_hbm, cot), (w2_hbm, w2), (w1_hbm, w1)))
    ]
    for copy in loads:
        copy.start()
    me = lax.axis_index("tiles")
    xpos = lax.axis_index("members")
    core = lax.rem(me, 2)
    ypos = lax.rem(me // 2, 4)
    zpos = me // 8
    pos = {"x": xpos, "y": ypos, "z": zpos}
    ring = zpos * (1 - core) + ypos * core
    other = ypos * (1 - core) + zpos * core

    def tid(z, y, c):
        return (z * 4 + y) * 2 + c

    partner = tid(zpos, ypos, 1 - core)

    def wrap(v):
        return lax.rem(v, 4)

    barrier = pltpu.get_barrier_semaphore()
    pl.semaphore_signal(barrier, inc=1, device_id={"tiles": partner}, device_id_type=MESH)
    for d in range(1, 4):
        for c in range(2):
            pl.semaphore_signal(barrier, inc=1, device_id={"tiles": tid(wrap(zpos + d), ypos, c)}, device_id_type=MESH)
            pl.semaphore_signal(barrier, inc=1, device_id={"tiles": tid(zpos, wrap(ypos + d), c)}, device_id_type=MESH)
        pl.semaphore_signal(barrier, inc=1, device_id={"members": wrap(xpos + d)}, device_id_type=MESH)

    r_i = lax.broadcasted_iota(jnp.int32, (128, 1024), 0)
    c_i = lax.broadcasted_iota(jnp.int32, (128, 1024), 1)
    e_i = r_i // 32
    k_i = r_i - e_i * 32
    want = jnp.where(e_i == 0, k_i, jnp.where(e_i == 1, 992 + k_i, jnp.where(e_i == 2, 32 * k_i, 32 * k_i + 31)))
    pickrow[...] = jnp.where(c_i == want, 1.0, 0.0).astype(BF16)
    m_r = lax.broadcasted_iota(jnp.int32, (288, 96), 0)
    m_c = lax.broadcasted_iota(jnp.int32, (288, 96), 1)
    m_b = m_r // 96
    m_t = (m_r - m_b * 96) // 32
    m_j = m_r - m_b * 96 - m_t * 32 + m_b - 1
    inside = (m_j >= 0) & (m_j < 32)
    mats[0] = jnp.where(inside & (m_c == m_t * 32 + m_j), 1.0, 0.0)
    mats[1] = jnp.where(inside & (m_c == m_t * 32 + 31 - m_j), 1.0, 0.0)
    tile_of = m_t

    pl.semaphore_wait(barrier, 16)

    def remote(src, dst, ssem, rsem, target):
        return pltpu.make_async_remote_copy(
            src_ref=src, dst_ref=dst, send_sem=ssem, recv_sem=rsem,
            device_id={"tiles": target}, device_id_type=MESH,
        )

    def remote_x(src, dst, ssem, rsem, target):
        return pltpu.make_async_remote_copy(
            src_ref=src, dst_ref=dst, send_sem=ssem, recv_sem=rsem,
            device_id={"members": target}, device_id_type=MESH,
        )

    sends = []

    def launch(make):
        make().start()
        sends.append(make)

    for d in range(1, 4):
        launch(lambda d=d: remote(tab.at[0], tabv.at[ypos * 2 + core], tab_s.at[d - 1], tab_r.at[ypos * 2 + core], tid(zpos, wrap(ypos + d), 0)))
        launch(lambda d=d: remote(tab.at[1], tabv.at[zpos * 2 + core], tab_s.at[d + 2], tab_r.at[zpos * 2 + core], tid(wrap(zpos + d), ypos, 1)))
    slot_p = (ypos * core + zpos * (1 - core)) * 2 + core
    launch(lambda: remote(tab.at[1 - core], tabv.at[slot_p], tab_s.at[6], tab_r.at[slot_p], partner))
    tab_own = pltpu.make_async_copy(tab.at[core], tabv.at[other * 2 + core], loc_sem.at[0])
    tab_own.start()

    def dot(a, b):
        return jnp.dot(a, b, preferred_element_type=F32)

    def dot_nt(a, b):
        return lax.dot_general(a, b, (((1,), (1,)), ((), ())), preferred_element_type=F32)

    def dot_tn(a, b):
        return lax.dot_general(a, b, (((0,), (0,)), ((), ())), preferred_element_type=F32)

    def take_edges(get, which):
        for t in range(3):
            picked = dot(pickrow[...], get(t)).astype(BF16)
            for e in range(4):
                edges[which, e, t * 32:t * 32 + 32, :] = picked[e * 32:e * 32 + 32]

    def put_edge(n, t, e, value):
        edge_out[n, 0, t * 4 + e] = value[:, 0:128]
        edge_out[n, 1, t * 4 + e] = value[:, 128:256]

    def put_edges(n, which):
        for t in range(3):
            for e in range(4):
                put_edge(n, t, e, edges[which, e, t * 32:t * 32 + 32, :])

    def send_edges(n):
        for d in range(1, 4):
            launch(lambda d=d: remote(edge_out.at[n, 0], ag[n].at[pl.ds((zpos * 2 + core) * 12, 12)], ag_s.at[n, d - 1], ag_r.at[n, zpos * 2 + core], tid(wrap(zpos + d), ypos, 0)))
            launch(lambda d=d: remote(edge_out.at[n, 1], ag[n].at[pl.ds((ypos * 2 + core) * 12, 12)], ag_s.at[n, d + 2], ag_r.at[n, ypos * 2 + core], tid(zpos, wrap(ypos + d), 1)))
        slot = (zpos * core + ypos * (1 - core)) * 2 + core
        launch(lambda: remote(edge_out.at[n, 1 - core], ag[n].at[pl.ds(slot * 12, 12)], ag_s.at[n, 6], ag_r.at[n, slot], partner))
        own = pltpu.make_async_copy(edge_out.at[n, core], ag[n].at[pl.ds((ring * 2 + core) * 12, 12)], loc_sem.at[1])
        own.start()
        own.wait()

    def forward(n):
        def wait(slot):
            remote(edge_out.at[n, 0], ag[n].at[pl.ds(slot * 12, 12)], ag_s.at[n, 0], ag_r.at[n, slot], partner).wait_recv()

        for d in range(1, 4):
            for c in range(2):
                wait(wrap(ring + d) * 2 + c)
        wait(ring * 2 + 1 - core)

        def choose(q, carry):
            for k in range(12):
                pick[n, q, k] = ag[n][tabs[q, 0, k]]
            return carry

        lax.fori_loop(0, 8, choose, 0)

        def one(d, c):
            p = wrap(other + d)
            target = tid(zpos * (1 - core) + p * core, p * (1 - core) + ypos * core, c)
            return remote(pick.at[n, p * 2 + c], got[n].at[core, other], pk_s.at[n, d * 2 + c - 2], pk_r.at[n, core * 4 + other], target)

        for d in range(1, 4):
            for c in range(2):
                launch(lambda d=d, c=c: one(d, c))
        launch(lambda: remote(pick.at[n, other * 2 + 1 - core], got[n].at[core, other], pk_s.at[n, 6], pk_r.at[n, core * 4 + other], partner))
        own = pltpu.make_async_copy(pick.at[n, other * 2 + core], got[n].at[core, other], loc_sem.at[2])
        own.start()
        own.wait()

    def arrive(n):
        def wait(h, p):
            remote(pick.at[n, 0], got[n].at[h, p], pk_s.at[n, 0], pk_r.at[n, h * 4 + p], partner).wait_recv()

        for d in range(1, 4):
            wait(0, wrap(ypos + d))
            wait(1, wrap(zpos + d))
        wait(1 - core, zpos * (1 - core) + ypos * core)

    def received(n, e):
        rows = []
        for t in range(3):
            k = t * 4 + e
            rows.append(jnp.concatenate([got[n][0, loc[0, k], k], got[n][1, loc[1, k], k]], axis=1))
        return jnp.concatenate(rows, axis=0)

    def turned(e, low, high):
        flip = jnp.where(tile_of == 0, loc[2, e], jnp.where(tile_of == 1, loc[2, 4 + e], loc[2, 8 + e]))[low:high]
        return jnp.where(flip == 1, mats[1, low:high], mats[0, low:high]).astype(BF16)

    def take_seams(n):
        for e in range(4):
            both = dot(turned(e, 0, 288), received(n, e)).astype(BF16)
            for b in range(3):
                seams[e, :, b * 256:b * 256 + 256] = both[b * 96:b * 96 + 96]

    jj = lax.rem(lax.broadcasted_iota(jnp.int32, (128, 256), 0), 32)

    def put3(dst, t, r, x):
        row = pl.multiple_of(32 + r * 128, 32)
        dst[t, pl.ds(row, 128), 256:512] = x.astype(BF16)
        dst[t, pl.ds(row, 128), 0:256] = jnp.where(jj == 0, 0.0, pltpu.roll(x, 1, 0)).astype(BF16)
        dst[t, pl.ds(row, 128), 512:768] = jnp.where(jj == 31, 0.0, pltpu.roll(x, 127, 0)).astype(BF16)

    def each_chunk(body):
        def step(i, carry):
            t = i // 8
            body(t, i - t * 8)
            return carry

        lax.fori_loop(0, 24, step, 0)

    def conv3(x3, weight, store, after=()):
        parts = 1024 // ROWS

        def step(i, carry):
            t = i // parts
            r = (i - t * parts) * ROWS
            acc = dot(x3[t, pl.ds(pl.multiple_of(r, 32), ROWS), :], weight(0))
            acc = acc + dot(x3[t, pl.ds(pl.multiple_of(r + 32, 32), ROWS), :], weight(1))
            acc = acc + dot(x3[t, pl.ds(pl.multiple_of(r + 64, 32), ROWS), :], weight(2))
            store(t, pl.multiple_of(r, 128), acc)
            for at, do in after:
                pl.when(i == at)(do)
            return carry

        lax.fori_loop(0, 3 * parts, step, 0)

    def edge_weight(w, e):
        return [w[0, 0], w[0, 1], w[0, 2]] if e == 0 else [w[2, 0], w[2, 1], w[2, 2]] if e == 1 else [w[0, 0], w[1, 0], w[2, 0]] if e == 2 else [w[0, 2], w[1, 2], w[2, 2]]

    eight = lax.broadcasted_iota(jnp.int32, (8, 256), 0)

    def add_edges(dst, value_of):
        for t in range(3):
            dst[t, 0:32, :] += value_of[0, t * 32:t * 32 + 32, :]
            dst[t, 992:1024, :] += value_of[1, t * 32:t * 32 + 32, :]

        def step(i, carry):
            for t in range(3):
                row = pl.multiple_of(i * 32, 8)
                line = jnp.broadcast_to(value_of[2, pl.ds(t * 32 + i, 1), :], (8, 256))
                dst[t, pl.ds(row, 8), :] += jnp.where(eight == 0, line, 0.0)
                row = pl.multiple_of(i * 32 + 24, 8)
                line = jnp.broadcast_to(value_of[3, pl.ds(t * 32 + i, 1), :], (8, 256))
                dst[t, pl.ds(row, 8), :] += jnp.where(eight == 7, line, 0.0)
            return carry

        lax.fori_loop(0, 32, step, 0)

    def seam_conv(w, dst):
        for e in range(4):
            ws = edge_weight(w, e)
            corr[e] = dot(seams[e, :, 0:256], ws[0]) + dot(seams[e, :, 256:512], ws[1]) + dot(seams[e, :, 512:768], ws[2])
        add_edges(dst, corr)

    def rim_add(n, dst):
        for e in range(4):
            corr[e] = dot(turned(e, 96, 192), received(n, e))
        add_edges(dst, corr)

    def rims(which, w, n):
        shift = mats[0].astype(BF16)
        for e in range(4):
            ws = edge_weight(w, e)
            rimrows[...] = dot(shift, edges[which, e]).astype(BF16)
            value = dot_nt(rimrows[192:288], ws[0]) + dot_nt(rimrows[96:192], ws[1]) + dot_nt(rimrows[0:96], ws[2])
            value = value.astype(BF16)
            for t in range(3):
                put_edge(n, t, e, value[t * 32:t * 32 + 32])

    def transpose_tiles(x3):
        eye = jnp.where(lax.broadcasted_iota(jnp.int32, (256, 256), 0) == lax.broadcasted_iota(jnp.int32, (256, 256), 1), 1.0, 0.0).astype(BF16)
        for t in range(3):
            xt[t] = dot_nt(eye, x3[t, 32:1056, 256:512]).astype(BF16)

    def turn_weight(w):
        for a in range(3):
            for b in range(3):
                wt[a, b * 256:b * 256 + 256, :] = w[2 - a, 2 - b].T

    def grad_inner(g3, dst):
        def step(i, carry):
            al = i // 3
            be = i - al * 3
            value = None
            for t in range(3):
                part = dot(xt[t], g3[t, pl.ds(pl.multiple_of(al * 32, 32), 1024), pl.ds(pl.multiple_of(be * 256, 256), 256)])
                value = part if value is None else value + part
            for h in range(2):
                dst[h, :, :, 8 - i] = value[:, h * 128:h * 128 + 128].reshape(4, 4, 16, 128)
            return carry

        lax.fori_loop(0, 9, step, 0)

    def grad_seams(which, dst):
        for e in range(4):
            value = dot_tn(seams[e], edges[which, e])
            for b in range(3):
                ab = (b, 6 + b, 3 * b, 3 * b + 2)[e]
                for h in range(2):
                    dst[h, :, :, ab] += value[b * 256:b * 256 + 256, h * 128:h * 128 + 128].reshape(4, 4, 16, 128)

    def along(axis, p, src, dst, ssem, rsem):
        if axis == "x":
            return remote_x(src, dst, ssem, rsem, p)
        return remote(src, dst, ssem, rsem, tid(zpos, p, core) if axis == "y" else tid(p, ypos, core))

    def swap(u, axis, base, src_of, dst_of):
        mine = pos[axis]
        for d in range(1, 4):
            def make(d=d):
                p = wrap(pos[axis] + d)
                return along(axis, p, src_of(p), dst_of(pos[axis]), ar_s.at[u, base + d - 1], ar_r.at[u, base + pos[axis]])

            launch(make)

    def swapped(u, axis, base, src_of, dst_of):
        for d in range(1, 4):
            p = wrap(pos[axis] + d)
            along(axis, p, src_of(p), dst_of(p), ar_s.at[u, base], ar_r.at[u, base + p]).wait_recv()

    def core_args(u):
        return (snd.at[u], rcore.at[u], ar_s.at[u, 0], ar_r.at[u, 0], partner)

    def first_args(u, r):
        return (u, ORDER[r][0], 1, lambda p: sx.at[u, p], lambda p: rx.at[u, p])

    def second_args(u, r):
        return (u, ORDER[r][1], 5, lambda p: sy.at[u, p], lambda p: ry.at[u, p])

    def third_args(u, r):
        return (u, ORDER[r][2], 9, lambda p: sz.at[u], lambda p: rz.at[u, p])

    def back_second_args(u, r):
        return (u, ORDER[r][1], 13, lambda p: full.at[u, core, pos[ORDER[r][0]], pos[ORDER[r][1]]], lambda p: full.at[u, core, pos[ORDER[r][0]], p])

    def back_first_args(u, r):
        return (u, ORDER[r][0], 17, lambda p: full.at[u, core, pos[ORDER[r][0]]], lambda p: full.at[u, core, p])

    def step_core(g):
        for r in range(3):
            u = g * 3 + r
            snd[u] = grads[g][1 - core, :, :, 3 * r:3 * r + 3].astype(BF16)
            launch(lambda u=u: remote(*core_args(u)))

    def step_first(g):
        for r in range(3):
            u = g * 3 + r
            remote(*core_args(u)).wait_recv()
            sx[u] = (grads[g][core, :, :, 3 * r:3 * r + 3] + rcore[u].astype(F32)).astype(BF16)
            swap(*first_args(u, r))

    def step_second(g):
        for r in range(3):
            u = g * 3 + r
            swapped(*first_args(u, r))
            mine = pos[ORDER[r][0]]
            total = grads[g][core, mine, :, 3 * r:3 * r + 3] + rcore[u, mine].astype(F32)
            for d in range(1, 4):
                total = total + rx[u, wrap(mine + d)].astype(F32)
            sy[u] = total.astype(BF16)
            swap(*second_args(u, r))

    def step_third(g):
        for r in range(3):
            u = g * 3 + r
            swapped(*second_args(u, r))
            mine = pos[ORDER[r][1]]
            total = sy[u, mine].astype(F32)
            for d in range(1, 4):
                total = total + ry[u, wrap(mine + d)].astype(F32)
            sz[u] = total
            swap(*third_args(u, r))

    def step_back_second(g):
        for r in range(3):
            u = g * 3 + r
            swapped(*third_args(u, r))
            total = sz[u]
            mine = pos[ORDER[r][2]]
            rz[u, mine] = total
            total = (rz[u, 0] + rz[u, 1]) + (rz[u, 2] + rz[u, 3])
            full[u, core, pos[ORDER[r][0]], pos[ORDER[r][1]]] = total.astype(BF16)
            swap(*back_second_args(u, r))

    def step_back_first(g):
        for r in range(3):
            u = g * 3 + r
            swapped(*back_second_args(u, r))
            swap(*back_first_args(u, r))

    def last_args(u, h):
        return (full.at[u, h], full.at[u, h], ar_s.at[u, 21], ar_r.at[u, 21], partner)

    def step_back_core(g):
        for r in range(3):
            u = g * 3 + r
            swapped(*back_first_args(u, r))
            launch(lambda u=u: remote(*last_args(u, core)))

    def step_end(g):
        for r in range(3):
            u = g * 3 + r
            remote(*last_args(u, 1 - core)).wait_recv()
            for b in range(3):
                for h in range(2):
                    gouts[g][3 * r + b, :, h * 128:h * 128 + 128] = full[u, h, :, :, b].reshape(256, 128)

    loads[0].wait()
    take_edges(lambda t: feat[t].reshape(1024, 256), 0)
    put_edges(0, 0)
    send_edges(0)
    loads[1].wait()
    loads[2].wait()
    take_edges(lambda t: cot[t].reshape(1024, 256), 1)
    rims(1, w2, 1)
    send_edges(1)

    for x3 in (fa3, c3, d3):
        x3[:, 0:32, :] = jnp.zeros((3, 32, 768), BF16)
        x3[:, 1056:1088, :] = jnp.zeros((3, 32, 768), BF16)

    def load_feat(t, r):
        put3(fa3, t, r, feat[t, pl.ds(r * 4, 4)].reshape(128, 256).astype(F32))

    def load_cot(t, r):
        put3(c3, t, r, cot[t, pl.ds(r * 4, 4)].reshape(128, 256).astype(F32))

    each_chunk(load_feat)
    for d in range(1, 4):
        for c in range(2):
            slot = wrap(other + d) * 2 + c
            remote(tab.at[0], tabv.at[slot], tab_s.at[0], tab_r.at[slot], partner).wait_recv()
    slot = other * 2 + 1 - core
    remote(tab.at[0], tabv.at[slot], tab_s.at[0], tab_r.at[slot], partner).wait_recv()
    tab_own.wait()
    to_smem = pltpu.make_async_copy(tabv, tabs, loc_sem.at[3])
    to_smem.start()
    to_smem.wait()

    def store_pre(t, r, acc):
        pre[t, pl.ds(r, ROWS), :] = acc

    def store_dact(t, r, acc):
        dact[t, pl.ds(r, ROWS), :] = acc

    loads[3].wait()
    conv3(fa3, lambda a: w1[a].reshape(768, 256), store_pre)
    forward(0)
    each_chunk(load_cot)
    turn_weight(w2)
    forward(1)
    conv3(c3, lambda a: wt[a], store_dact)
    transpose_tiles(fa3)
    turn_weight(w1)
    arrive(0)
    take_seams(0)
    seam_conv(w1, pre)

    def activate(t, r):
        row = pl.multiple_of(r * 128, 128)
        u = pre[t, pl.ds(row, 128), :]
        s = 1.0 / (1.0 + jnp.exp(-u))
        put3(fa3, t, r, (u * s).astype(BF16).astype(F32))
        pre[t, pl.ds(row, 128), :] = s * (1.0 + u * (1.0 - s))

    each_chunk(activate)

    take_edges(lambda t: fa3[t, 32:1056, 256:512], 2)
    put_edges(2, 2)
    send_edges(2)
    arrive(1)
    rim_add(1, dact)

    def slope(t, r):
        row = pl.multiple_of(r * 128, 128)
        d = dact[t, pl.ds(row, 128), :] * pre[t, pl.ds(row, 128), :]
        put3(d3, t, r, d.astype(BF16).astype(F32))

    each_chunk(slope)
    take_edges(lambda t: d3[t, 32:1056, 256:512], 0)
    rims(0, w1, 3)
    send_edges(3)
    grad_inner(d3, grad1)
    grad_seams(0, grad1)
    step_core(0)
    forward(2)
    transpose_tiles(fa3)
    step_first(0)
    grad_inner(c3, grad2)
    step_second(0)
    forward(3)
    arrive(2)
    take_seams(2)
    grad_seams(1, grad2)
    step_core(1)
    step_third(0)

    def after_a():
        step_first(1)
        step_back_second(0)

    def after_b():
        step_second(1)
        step_back_first(0)

    def after_c():
        step_third(1)
        step_back_core(0)

    conv3(fa3, lambda a: w2[a].reshape(768, 256), store_pre, ((1, after_a), (4, after_b)))
    seam_conv(w2, pre)
    after_c()

    def finish_out(t, r):
        row = pl.multiple_of(r * 128, 128)
        out[t, pl.ds(row, 128), :] = pre[t, pl.ds(row, 128), :].astype(BF16)

    def finish_gfeat(t, r):
        row = pl.multiple_of(r * 128, 128)
        gfeat[t, pl.ds(row, 128), :] = dact[t, pl.ds(row, 128), :].astype(BF16)

    each_chunk(finish_out)
    conv3(d3, lambda a: wt[a], store_dact, ((0, lambda: step_back_second(1)), (2, lambda: step_back_first(1)), (5, lambda: step_back_core(1))))
    step_end(0)
    arrive(3)
    rim_add(3, dact)
    each_chunk(finish_gfeat)
    step_end(1)
    for make in sends:
        make().wait_send()


def on_device(features, conv_one, conv_two, cotangent, neighbour_tile, rotation):
    cells_all = lax.axis_size("members") * lax.axis_size("tiles") * 3 * 1024
    factor = 1.0 / math.sqrt(cells_all)
    source = (4 * neighbour_tile + rotation % 4).reshape(12)
    device = source // 12
    z_of, y_of, c_of, row = device // 8, device // 2 % 4, device % 2, source % 12
    tab = jnp.stack([(z_of * 2 + c_of) * 12 + row, (y_of * 2 + c_of) * 12 + row])
    tab = jnp.broadcast_to(jnp.pad(tab, ((0, 0), (0, 116)))[:, None], (2, 8, 128))
    loc = jnp.stack([y_of, z_of, (rotation // 4).reshape(12)])
    vmem = pl.BlockSpec(memory_space=pltpu.VMEM)
    dma = pltpu.SemaphoreType.DMA
    out, gfeat, gout1, gout2 = pl.pallas_call(
        kernel,
        out_shape=(
            jax.ShapeDtypeStruct((3, 1024, 256), BF16),
            jax.ShapeDtypeStruct((3, 1024, 256), BF16),
            jax.ShapeDtypeStruct((9, 256, 256), BF16),
            jax.ShapeDtypeStruct((9, 256, 256), BF16),
        ),
        in_specs=[pl.BlockSpec(memory_space=pl.ANY)] * 4 + [vmem] + [pl.BlockSpec(memory_space=pltpu.SMEM)],
        out_specs=(vmem,) * 4,
        scratch_shapes=[
            pltpu.VMEM((3, 32, 32, 256), BF16),
            pltpu.VMEM((3, 32, 32, 256), BF16),
            pltpu.VMEM((3, 3, 256, 256), BF16),
            pltpu.VMEM((3, 3, 256, 256), BF16),
            pltpu.VMEM((3, 1088, 768), BF16),
            pltpu.VMEM((3, 1088, 768), BF16),
            pltpu.VMEM((3, 1088, 768), BF16),
            pltpu.VMEM((3, 768, 256), BF16),
            pltpu.VMEM((3, 1024, 256), F32),
            pltpu.VMEM((3, 1024, 256), F32),
            pltpu.VMEM((3, 256, 1024), BF16),
            pltpu.VMEM((2, 4, 4, 9, 16, 128), F32),
            pltpu.VMEM((2, 4, 4, 9, 16, 128), F32),
            pltpu.VMEM((4, 96, 768), BF16),
            pltpu.VMEM((3, 4, 96, 256), BF16),
            pltpu.VMEM((288, 256), BF16),
            pltpu.VMEM((4, 96, 256), F32),
            pltpu.VMEM((2, 288, 96), F32),
            pltpu.VMEM((128, 1024), BF16),
            pltpu.VMEM((4, 2, 12, 32, 128), BF16),
            *[pltpu.VMEM((96, 32, 128), BF16)] * 4,
            pltpu.VMEM((4, 8, 12, 32, 128), BF16),
            *[pltpu.VMEM((2, 4, 12, 32, 128), BF16)] * 4,
            pltpu.VMEM((8, 8, 128), jnp.int32),
            pltpu.SMEM((8, 8, 128), jnp.int32),
            pltpu.VMEM((6, 4, 4, 3, 16, 128), BF16),
            pltpu.VMEM((6, 4, 4, 3, 16, 128), BF16),
            pltpu.VMEM((6, 4, 4, 3, 16, 128), BF16),
            pltpu.VMEM((6, 4, 4, 3, 16, 128), BF16),
            pltpu.VMEM((6, 4, 3, 16, 128), BF16),
            pltpu.VMEM((6, 4, 3, 16, 128), BF16),
            pltpu.VMEM((6, 3, 16, 128), F32),
            pltpu.VMEM((6, 4, 3, 16, 128), F32),
            pltpu.VMEM((6, 2, 4, 4, 3, 16, 128), BF16),
            dma((7,)),
            dma((8,)),
            dma((4, 7)),
            dma((4, 8)),
            dma((4, 7)),
            dma((4, 8)),
            dma((6, 22)),
            dma((6, 22)),
            dma((4,)),
            dma((4,)),
        ],
        compiler_params=pltpu.CompilerParams(
            collective_id=0, has_side_effects=True, vmem_limit_bytes=67043328
        ),
    )(features[0], cotangent[0], conv_one, conv_two, tab, loc)

    def whole(total):
        return (total.astype(F32) * factor).reshape(3, 3, 256, 256)

    shape = features.shape
    return (out.reshape(shape), gfeat.reshape(shape), whole(gout1), whole(gout2))


def solution(mesh):
    placed = (
        P("members", "tiles", None, None, None),
        P(),
        P(),
        P("members", "tiles", None, None, None),
        P("tiles", None),
        P("tiles", None),
    )
    return jax.shard_map(
        on_device,
        mesh=mesh,
        in_specs=placed,
        out_specs=(
            P("members", "tiles", None, None, None),
            P("members", "tiles", None, None, None),
            P(),
            P(),
        ),
        check_vma=False,
    )
```

```python
import functools
import math

import jax
import jax.numpy as jnp
from jax import lax
from jax.experimental import pallas as pl
from jax.experimental.pallas import tpu as pltpu
from jax.sharding import PartitionSpec as P

MESH = pl.DeviceIdType.MESH
F32 = jnp.float32
BF16 = jnp.bfloat16
ROWS = 512


ORDER = ("xyz", "yzx", "zxy")


def kernel(
    feat_hbm, cot_hbm, w1_hbm, w2_hbm, near_v, turn_v, near, turn,
    out_hbm, gfeat_hbm, gout1_hbm, gout2_hbm,
    feat, cot, w1, w2, out, gfeat, gout1, gout2,
    fa3, c3, d3, wt, pre, dact, xt, grad1, grad2, seams, edges, rimrows, corr, mats, pickrow,
    edge_out, ag0, ag1, ag2, ag3, pick, got0, got1, got2, got3, tab, tabw, tabv, tabs,
    snd, rcore, sx, rx, sy, ry, sz, rz, full,
    tab_s, tab_r, ag_s, ag_r, pk_s, pk_r, ar_s, ar_r, loc_sem, in_sem, out_sem,
):
    ag = (ag0, ag1, ag2, ag3)
    got = (got0, got1, got2, got3)
    grads = (grad1, grad2)
    gouts = (gout1, gout2)
    loads = [
        pltpu.make_async_copy(src, dst, in_sem.at[i])
        for i, (src, dst) in enumerate(((feat_hbm, feat), (cot_hbm, cot), (w2_hbm, w2), (w1_hbm, w1)))
    ]
    for copy in loads:
        copy.start()
    stores = [
        pltpu.make_async_copy(src, dst, out_sem.at[i])
        for i, (src, dst) in enumerate(((out, out_hbm), (gfeat, gfeat_hbm), (gout1, gout1_hbm), (gout2, gout2_hbm)))
    ]
    me = lax.axis_index("tiles")
    xpos = lax.axis_index("members")
    core = lax.rem(me, 2)
    ypos = lax.rem(me // 2, 4)
    zpos = me // 8
    pos = {"x": xpos, "y": ypos, "z": zpos}
    ring = zpos * (1 - core) + ypos * core
    other = ypos * (1 - core) + zpos * core

    def tid(z, y, c):
        return (z * 4 + y) * 2 + c

    partner = tid(zpos, ypos, 1 - core)

    def wrap(v):
        return lax.rem(v, 4)

    barrier = pltpu.get_barrier_semaphore()
    pl.semaphore_signal(barrier, inc=1, device_id={"tiles": partner}, device_id_type=MESH)
    for d in range(1, 4):
        for c in range(2):
            pl.semaphore_signal(barrier, inc=1, device_id={"tiles": tid(wrap(zpos + d), ypos, c)}, device_id_type=MESH)
            pl.semaphore_signal(barrier, inc=1, device_id={"tiles": tid(zpos, wrap(ypos + d), c)}, device_id_type=MESH)
        pl.semaphore_signal(barrier, inc=1, device_id={"members": wrap(xpos + d)}, device_id_type=MESH)

    r_i = lax.broadcasted_iota(jnp.int32, (128, 1024), 0)
    c_i = lax.broadcasted_iota(jnp.int32, (128, 1024), 1)
    e_i = r_i // 32
    k_i = r_i - e_i * 32
    want = jnp.where(e_i == 0, k_i, jnp.where(e_i == 1, 992 + k_i, jnp.where(e_i == 2, 32 * k_i, 32 * k_i + 31)))
    pickrow[...] = jnp.where(c_i == want, 1.0, 0.0).astype(BF16)
    m_r = lax.broadcasted_iota(jnp.int32, (288, 96), 0)
    m_c = lax.broadcasted_iota(jnp.int32, (288, 96), 1)
    m_b = m_r // 96
    m_t = (m_r - m_b * 96) // 32
    m_j = m_r - m_b * 96 - m_t * 32 + m_b - 1
    inside = (m_j >= 0) & (m_j < 32)
    mats[0] = jnp.where(inside & (m_c == m_t * 32 + m_j), 1.0, 0.0)
    mats[1] = jnp.where(inside & (m_c == m_t * 32 + 31 - m_j), 1.0, 0.0)
    tile_of = m_t

    def remote(src, dst, ssem, rsem, target):
        return pltpu.make_async_remote_copy(
            src_ref=src, dst_ref=dst, send_sem=ssem, recv_sem=rsem,
            device_id={"tiles": target}, device_id_type=MESH,
        )

    def remote_x(src, dst, ssem, rsem, target):
        return pltpu.make_async_remote_copy(
            src_ref=src, dst_ref=dst, send_sem=ssem, recv_sem=rsem,
            device_id={"members": target}, device_id_type=MESH,
        )

    sends = []

    def launch(make):
        make().start()
        sends.append(make)

    def fill_tables():
        way = turn_v[...]
        src = 4 * near_v[...] + (way & 3)
        device = (src * 43691) >> 19
        z_of, y_of, c_of = device >> 3, (device >> 1) & 3, device & 1
        row = src - 12 * device
        for h, at in enumerate((z_of, y_of)):
            tabw[h] = jnp.zeros((8, 128), jnp.int32)
            tabw[h, 0:3, 0:4] = (at * 2 + c_of) * 12 + row
            wide = tabw[h]
            tab[h] = wide[0:1] + pltpu.roll(wide, 4, 1)[1:2] + pltpu.roll(wide, 8, 1)[2:3]

    def dot(a, b):
        return jnp.dot(a, b, preferred_element_type=F32)

    def dot_nt(a, b):
        return lax.dot_general(a, b, (((1,), (1,)), ((), ())), preferred_element_type=F32)

    def dot_tn(a, b):
        return lax.dot_general(a, b, (((0,), (0,)), ((), ())), preferred_element_type=F32)

    def take_edges(get, which):
        for t in range(3):
            picked = dot(pickrow[...], get(t)).astype(BF16)
            for e in range(4):
                edges[which, e, t * 32:t * 32 + 32, :] = picked[e * 32:e * 32 + 32]

    def put_edge(n, t, e, value):
        edge_out[n, 0, t * 4 + e] = value[:, 0:128]
        edge_out[n, 1, t * 4 + e] = value[:, 128:256]

    def put_edges(n, which):
        for t in range(3):
            for e in range(4):
                put_edge(n, t, e, edges[which, e, t * 32:t * 32 + 32, :])

    def send_edges(n):
        for d in range(1, 4):
            launch(lambda d=d: remote(edge_out.at[n, 0], ag[n].at[pl.ds((zpos * 2 + core) * 12, 12)], ag_s.at[n, d - 1], ag_r.at[n, zpos * 2 + core], tid(wrap(zpos + d), ypos, 0)))
            launch(lambda d=d: remote(edge_out.at[n, 1], ag[n].at[pl.ds((ypos * 2 + core) * 12, 12)], ag_s.at[n, d + 2], ag_r.at[n, ypos * 2 + core], tid(zpos, wrap(ypos + d), 1)))
        slot = (zpos * core + ypos * (1 - core)) * 2 + core
        launch(lambda: remote(edge_out.at[n, 1 - core], ag[n].at[pl.ds(slot * 12, 12)], ag_s.at[n, 6], ag_r.at[n, slot], partner))
        own = pltpu.make_async_copy(edge_out.at[n, core], ag[n].at[pl.ds((ring * 2 + core) * 12, 12)], loc_sem.at[1])
        own.start()
        own.wait()

    def forward(n):
        def wait(slot):
            remote(edge_out.at[n, 0], ag[n].at[pl.ds(slot * 12, 12)], ag_s.at[n, 0], ag_r.at[n, slot], partner).wait_recv()

        for d in range(1, 4):
            for c in range(2):
                wait(wrap(ring + d) * 2 + c)
        wait(ring * 2 + 1 - core)

        def choose(q, carry):
            for k in range(12):
                pick[n, q, k] = ag[n][tabs[q, 0, k]]
            return carry

        lax.fori_loop(0, 8, choose, 0)

        def one(d, c):
            p = wrap(other + d)
            target = tid(zpos * (1 - core) + p * core, p * (1 - core) + ypos * core, c)
            return remote(pick.at[n, p * 2 + c], got[n].at[core, other], pk_s.at[n, d * 2 + c - 2], pk_r.at[n, core * 4 + other], target)

        for d in range(1, 4):
            for c in range(2):
                launch(lambda d=d, c=c: one(d, c))
        launch(lambda: remote(pick.at[n, other * 2 + 1 - core], got[n].at[core, other], pk_s.at[n, 6], pk_r.at[n, core * 4 + other], partner))
        own = pltpu.make_async_copy(pick.at[n, other * 2 + core], got[n].at[core, other], loc_sem.at[2])
        own.start()
        own.wait()

    def arrive(n):
        def wait(h, p):
            remote(pick.at[n, 0], got[n].at[h, p], pk_s.at[n, 0], pk_r.at[n, h * 4 + p], partner).wait_recv()

        for d in range(1, 4):
            wait(0, wrap(ypos + d))
            wait(1, wrap(zpos + d))
        wait(1 - core, zpos * (1 - core) + ypos * core)

    def source(k):
        way = turn[k // 4, k % 4]
        device = lax.div(4 * near[k // 4, k % 4] + lax.rem(way, 4), 12)
        return lax.rem(lax.div(device, 2), 4), lax.div(device, 8), lax.div(way, 4)

    def received(n, e):
        rows = []
        for t in range(3):
            k = t * 4 + e
            y_from, z_from, _ = source(k)
            rows.append(jnp.concatenate([got[n][0, y_from, k], got[n][1, z_from, k]], axis=1))
        return jnp.concatenate(rows, axis=0)

    def turned(e, low, high):
        flip = jnp.where(tile_of == 0, source(e)[2], jnp.where(tile_of == 1, source(4 + e)[2], source(8 + e)[2]))[low:high]
        return jnp.where(flip == 1, mats[1, low:high], mats[0, low:high]).astype(BF16)

    def take_seams(n):
        for e in range(4):
            both = dot(turned(e, 0, 288), received(n, e)).astype(BF16)
            for b in range(3):
                seams[e, :, b * 256:b * 256 + 256] = both[b * 96:b * 96 + 96]

    jj = lax.rem(lax.broadcasted_iota(jnp.int32, (128, 256), 0), 32)

    def put3(dst, t, r, x):
        row = pl.multiple_of(32 + r * 128, 32)
        dst[t, pl.ds(row, 128), 256:512] = x.astype(BF16)
        dst[t, pl.ds(row, 128), 0:256] = jnp.where(jj == 0, 0.0, pltpu.roll(x, 1, 0)).astype(BF16)
        dst[t, pl.ds(row, 128), 512:768] = jnp.where(jj == 31, 0.0, pltpu.roll(x, 127, 0)).astype(BF16)

    def each_chunk(body):
        def step(i, carry):
            t = i // 8
            body(t, i - t * 8)
            return carry

        lax.fori_loop(0, 24, step, 0)

    def conv3(x3, weight, store, after=()):
        parts = 1024 // ROWS

        def step(i, carry):
            t = i // parts
            r = (i - t * parts) * ROWS
            acc = dot(x3[t, pl.ds(pl.multiple_of(r, 32), ROWS), :], weight(0))
            acc = acc + dot(x3[t, pl.ds(pl.multiple_of(r + 32, 32), ROWS), :], weight(1))
            acc = acc + dot(x3[t, pl.ds(pl.multiple_of(r + 64, 32), ROWS), :], weight(2))
            store(t, pl.multiple_of(r, 128), acc)
            for at, do in after:
                pl.when(i == at)(do)
            return carry

        lax.fori_loop(0, 3 * parts, step, 0)

    def edge_weight(w, e):
        return [w[0, 0], w[0, 1], w[0, 2]] if e == 0 else [w[2, 0], w[2, 1], w[2, 2]] if e == 1 else [w[0, 0], w[1, 0], w[2, 0]] if e == 2 else [w[0, 2], w[1, 2], w[2, 2]]

    eight = lax.broadcasted_iota(jnp.int32, (8, 256), 0)

    def add_edges(dst, value_of):
        for t in range(3):
            dst[t, 0:32, :] += value_of[0, t * 32:t * 32 + 32, :]
            dst[t, 992:1024, :] += value_of[1, t * 32:t * 32 + 32, :]

        def step(i, carry):
            for t in range(3):
                row = pl.multiple_of(i * 32, 8)
                line = jnp.broadcast_to(value_of[2, pl.ds(t * 32 + i, 1), :], (8, 256))
                dst[t, pl.ds(row, 8), :] += jnp.where(eight == 0, line, 0.0)
                row = pl.multiple_of(i * 32 + 24, 8)
                line = jnp.broadcast_to(value_of[3, pl.ds(t * 32 + i, 1), :], (8, 256))
                dst[t, pl.ds(row, 8), :] += jnp.where(eight == 7, line, 0.0)
            return carry

        lax.fori_loop(0, 32, step, 0)

    def seam_conv(w, dst):
        for e in range(4):
            ws = edge_weight(w, e)
            corr[e] = dot(seams[e, :, 0:256], ws[0]) + dot(seams[e, :, 256:512], ws[1]) + dot(seams[e, :, 512:768], ws[2])
        add_edges(dst, corr)

    def rim_add(n, dst):
        for e in range(4):
            corr[e] = dot(turned(e, 96, 192), received(n, e))
        add_edges(dst, corr)

    def rims(which, w, n):
        shift = mats[0].astype(BF16)
        for e in range(4):
            ws = edge_weight(w, e)
            rimrows[...] = dot(shift, edges[which, e]).astype(BF16)
            value = dot_nt(rimrows[192:288], ws[0]) + dot_nt(rimrows[96:192], ws[1]) + dot_nt(rimrows[0:96], ws[2])
            value = value.astype(BF16)
            for t in range(3):
                put_edge(n, t, e, value[t * 32:t * 32 + 32])

    def transpose_tiles(x3):
        eye = jnp.where(lax.broadcasted_iota(jnp.int32, (256, 256), 0) == lax.broadcasted_iota(jnp.int32, (256, 256), 1), 1.0, 0.0).astype(BF16)
        for t in range(3):
            xt[t] = dot_nt(eye, x3[t, 32:1056, 256:512]).astype(BF16)

    def turn_weight(w):
        for a in range(3):
            for b in range(3):
                wt[a, b * 256:b * 256 + 256, :] = w[2 - a, 2 - b].T

    def grad_inner(g3, dst, after=()):
        def step(i, carry):
            al = i // 3
            be = i - al * 3
            value = None
            for t in range(3):
                part = dot(xt[t], g3[t, pl.ds(pl.multiple_of(al * 32, 32), 1024), pl.ds(pl.multiple_of(be * 256, 256), 256)])
                value = part if value is None else value + part
            for h in range(2):
                dst[h, :, :, 8 - i] = value[:, h * 128:h * 128 + 128].reshape(4, 4, 16, 128)
            for at, do in after:
                pl.when(i == at)(do)
            return carry

        lax.fori_loop(0, 9, step, 0)

    def grad_seams(which, dst):
        for e in range(4):
            value = dot_tn(seams[e], edges[which, e])
            for b in range(3):
                ab = (b, 6 + b, 3 * b, 3 * b + 2)[e]
                for h in range(2):
                    dst[h, :, :, ab] += value[b * 256:b * 256 + 256, h * 128:h * 128 + 128].reshape(4, 4, 16, 128)

    def along(axis, p, src, dst, ssem, rsem):
        if axis == "x":
            return remote_x(src, dst, ssem, rsem, p)
        return remote(src, dst, ssem, rsem, tid(zpos, p, core) if axis == "y" else tid(p, ypos, core))

    def swap(u, axis, base, src_of, dst_of):
        mine = pos[axis]
        for d in range(1, 4):
            def make(d=d):
                p = wrap(pos[axis] + d)
                return along(axis, p, src_of(p), dst_of(pos[axis]), ar_s.at[u, base + d - 1], ar_r.at[u, base + pos[axis]])

            launch(make)

    def swapped(u, axis, base, src_of, dst_of):
        for d in range(1, 4):
            p = wrap(pos[axis] + d)
            along(axis, p, src_of(p), dst_of(p), ar_s.at[u, base], ar_r.at[u, base + p]).wait_recv()

    def core_args(u):
        return (snd.at[u], rcore.at[u], ar_s.at[u, 0], ar_r.at[u, 0], partner)

    def first_args(u, r):
        return (u, ORDER[r][0], 1, lambda p: sx.at[u, p], lambda p: rx.at[u, p])

    def second_args(u, r):
        return (u, ORDER[r][1], 5, lambda p: sy.at[u, p], lambda p: ry.at[u, p])

    def third_args(u, r):
        return (u, ORDER[r][2], 9, lambda p: sz.at[u], lambda p: rz.at[u, p])

    def back_second_args(u, r):
        return (u, ORDER[r][1], 13, lambda p: full.at[u, core, pos[ORDER[r][0]], pos[ORDER[r][1]]], lambda p: full.at[u, core, pos[ORDER[r][0]], p])

    def back_first_args(u, r):
        return (u, ORDER[r][0], 17, lambda p: full.at[u, core, pos[ORDER[r][0]]], lambda p: full.at[u, core, p])

    def step_core(g):
        for r in range(3):
            u = g * 3 + r
            snd[u] = grads[g][1 - core, :, :, 3 * r:3 * r + 3].astype(BF16)
            launch(lambda u=u: remote(*core_args(u)))

    def step_first(g):
        for r in range(3):
            u = g * 3 + r
            remote(*core_args(u)).wait_recv()
            sx[u] = (grads[g][core, :, :, 3 * r:3 * r + 3] + rcore[u].astype(F32)).astype(BF16)
            swap(*first_args(u, r))

    def step_second(g):
        for r in range(3):
            u = g * 3 + r
            swapped(*first_args(u, r))
            mine = pos[ORDER[r][0]]
            total = grads[g][core, mine, :, 3 * r:3 * r + 3] + rcore[u, mine].astype(F32)
            for d in range(1, 4):
                total = total + rx[u, wrap(mine + d)].astype(F32)
            sy[u] = total.astype(BF16)
            swap(*second_args(u, r))

    def step_third(g):
        for r in range(3):
            u = g * 3 + r
            swapped(*second_args(u, r))
            mine = pos[ORDER[r][1]]
            total = sy[u, mine].astype(F32)
            for d in range(1, 4):
                total = total + ry[u, wrap(mine + d)].astype(F32)
            sz[u] = total
            swap(*third_args(u, r))

    def step_back_second(g):
        for r in range(3):
            u = g * 3 + r
            swapped(*third_args(u, r))
            total = sz[u]
            mine = pos[ORDER[r][2]]
            rz[u, mine] = total
            total = (rz[u, 0] + rz[u, 1]) + (rz[u, 2] + rz[u, 3])
            full[u, core, pos[ORDER[r][0]], pos[ORDER[r][1]]] = total.astype(BF16)
            swap(*back_second_args(u, r))

    def step_back_first(g):
        for r in range(3):
            u = g * 3 + r
            swapped(*back_second_args(u, r))
            swap(*back_first_args(u, r))

    def last_args(u, h):
        return (full.at[u, h], full.at[u, h], ar_s.at[u, 21], ar_r.at[u, 21], partner)

    def step_back_core(g):
        for r in range(3):
            u = g * 3 + r
            swapped(*back_first_args(u, r))
            launch(lambda u=u: remote(*last_args(u, core)))

    def step_end(g):
        for r in range(3):
            u = g * 3 + r
            remote(*last_args(u, 1 - core)).wait_recv()
            for b in range(3):
                for h in range(2):
                    gouts[g][3 * r + b, :, h * 128:h * 128 + 128] = full[u, h, :, :, b].reshape(256, 128)

    fill_tables()
    loads[0].wait()
    take_edges(lambda t: feat[t].reshape(1024, 256), 0)
    put_edges(0, 0)
    pl.semaphore_wait(barrier, 16)
    send_edges(0)

    for d in range(1, 4):
        launch(lambda d=d: remote(tab.at[0], tabv.at[ypos * 2 + core], tab_s.at[d - 1], tab_r.at[ypos * 2 + core], tid(zpos, wrap(ypos + d), 0)))
        launch(lambda d=d: remote(tab.at[1], tabv.at[zpos * 2 + core], tab_s.at[d + 2], tab_r.at[zpos * 2 + core], tid(wrap(zpos + d), ypos, 1)))
    slot_p = (ypos * core + zpos * (1 - core)) * 2 + core
    launch(lambda: remote(tab.at[1 - core], tabv.at[slot_p], tab_s.at[6], tab_r.at[slot_p], partner))
    tab_own = pltpu.make_async_copy(tab.at[core], tabv.at[other * 2 + core], loc_sem.at[0])
    tab_own.start()

    loads[1].wait()
    loads[2].wait()
    take_edges(lambda t: cot[t].reshape(1024, 256), 1)
    rims(1, w2, 1)
    send_edges(1)

    for x3 in (fa3, c3, d3):
        x3[:, 0:32, :] = jnp.zeros((3, 32, 768), BF16)
        x3[:, 1056:1088, :] = jnp.zeros((3, 32, 768), BF16)

    def load_feat(t, r):
        put3(fa3, t, r, feat[t, pl.ds(r * 4, 4)].reshape(128, 256).astype(F32))

    def load_cot(t, r):
        put3(c3, t, r, cot[t, pl.ds(r * 4, 4)].reshape(128, 256).astype(F32))

    each_chunk(load_feat)
    for d in range(1, 4):
        for c in range(2):
            slot = wrap(other + d) * 2 + c
            remote(tab.at[0], tabv.at[slot], tab_s.at[0], tab_r.at[slot], partner).wait_recv()
    slot = other * 2 + 1 - core
    remote(tab.at[0], tabv.at[slot], tab_s.at[0], tab_r.at[slot], partner).wait_recv()
    tab_own.wait()
    to_smem = pltpu.make_async_copy(tabv, tabs, loc_sem.at[3])
    to_smem.start()
    to_smem.wait()

    def store_pre(t, r, acc):
        pre[t, pl.ds(r, ROWS), :] = acc

    def store_dact(t, r, acc):
        dact[t, pl.ds(r, ROWS), :] = acc

    loads[3].wait()
    conv3(fa3, lambda a: w1[a].reshape(768, 256), store_pre, ((4, lambda: forward(0)),))
    each_chunk(load_cot)
    turn_weight(w2)
    conv3(c3, lambda a: wt[a], store_dact, ((1, lambda: forward(1)),))
    transpose_tiles(fa3)
    turn_weight(w1)
    arrive(0)
    take_seams(0)
    seam_conv(w1, pre)

    def activate(t, r):
        row = pl.multiple_of(r * 128, 128)
        u = pre[t, pl.ds(row, 128), :]
        s = 1.0 / (1.0 + jnp.exp(-u))
        put3(fa3, t, r, (u * s).astype(BF16).astype(F32))
        pre[t, pl.ds(row, 128), :] = s * (1.0 + u * (1.0 - s))

    each_chunk(activate)

    take_edges(lambda t: fa3[t, 32:1056, 256:512], 2)
    put_edges(2, 2)
    send_edges(2)
    arrive(1)
    rim_add(1, dact)

    def slope(t, r):
        row = pl.multiple_of(r * 128, 128)
        d = dact[t, pl.ds(row, 128), :] * pre[t, pl.ds(row, 128), :]
        put3(d3, t, r, d.astype(BF16).astype(F32))

    each_chunk(slope)
    take_edges(lambda t: d3[t, 32:1056, 256:512], 0)
    rims(0, w1, 3)
    send_edges(3)
    grad_inner(d3, grad1, ((3, lambda: forward(2)),))
    grad_seams(0, grad1)
    step_core(0)
    transpose_tiles(fa3)
    grad_inner(c3, grad2, ((1, lambda: step_first(0)), (3, lambda: forward(3))))
    arrive(2)
    take_seams(2)
    grad_seams(1, grad2)
    step_core(1)
    step_second(0)
    conv3(
        fa3, lambda a: w2[a].reshape(768, 256), store_pre,
        ((1, lambda: step_first(1)), (3, lambda: step_third(0)), (5, lambda: step_second(1))),
    )

    def finish_out(t, r):
        row = pl.multiple_of(r * 128, 128)
        out[t, pl.ds(row, 128), :] = pre[t, pl.ds(row, 128), :].astype(BF16)

    def finish_gfeat(t, r):
        row = pl.multiple_of(r * 128, 128)
        gfeat[t, pl.ds(row, 128), :] = dact[t, pl.ds(row, 128), :].astype(BF16)

    seam_conv(w2, pre)
    step_back_second(0)
    each_chunk(finish_out)
    stores[0].start()
    step_third(1)
    conv3(
        d3, lambda a: wt[a], store_dact,
        ((1, lambda: step_back_first(0)), (3, lambda: step_back_second(1))),
    )
    arrive(3)
    rim_add(3, dact)
    step_back_core(0)
    step_back_first(1)
    each_chunk(finish_gfeat)
    stores[1].start()
    step_end(0)
    stores[2].start()
    step_back_core(1)
    step_end(1)
    stores[3].start()
    for copy in stores:
        copy.wait()
    for make in sends:
        make().wait_send()


def results(factor, out_in, gfeat_in, g1_in, g2_in, out, gfeat, g1, g2, held_g, held, total, sem_in, sem_out):
    pieces = [(i, g_in, g, 768 * r) for r in range(3) for i, (g_in, g) in enumerate(((g1_in, g1), (g2_in, g2)))]
    gets = [
        pltpu.make_async_copy(g_in.at[pl.ds(row, 768)], held_g.at[i, pl.ds(row, 768)], sem_in.at[n])
        for n, (i, g_in, g, row) in enumerate(pieces)
    ]
    puts = [
        pltpu.make_async_copy(total.at[i, pl.ds(row, 768)], g.at[pl.ds(row, 768)], sem_out.at[n])
        for n, (i, g_in, g, row) in enumerate(pieces)
    ]
    fields = [(i, f_in, f, 1536 * r) for r in range(2) for i, (f_in, f) in enumerate(((out_in, out), (gfeat_in, gfeat)))]
    gets += [
        pltpu.make_async_copy(f_in.at[pl.ds(row, 1536)], held.at[i, pl.ds(row, 1536)], sem_in.at[6 + n])
        for n, (i, f_in, f, row) in enumerate(fields)
    ]
    puts += [
        pltpu.make_async_copy(held.at[i, pl.ds(row, 1536)], f.at[pl.ds(row, 1536)], sem_out.at[6 + n])
        for n, (i, f_in, f, row) in enumerate(fields)
    ]
    for copy in gets:
        copy.start()
    for n, (i, g_in, g, row) in enumerate(pieces):
        gets[n].wait()
        total[i, pl.ds(row, 768)] = held_g[i, pl.ds(row, 768)].astype(F32) * factor
        puts[n].start()
    for n in range(6, 10):
        gets[n].wait()
        puts[n].start()
    for copy in puts:
        copy.wait()


def on_device(features, conv_one, conv_two, cotangent, neighbour_tile, rotation):
    cells_all = lax.axis_size("members") * lax.axis_size("tiles") * 3 * 1024
    factor = 1.0 / math.sqrt(cells_all)
    vmem = pl.BlockSpec(memory_space=pltpu.VMEM)
    dma = pltpu.SemaphoreType.DMA
    out, gfeat, gout1, gout2 = pl.pallas_call(
        kernel,
        out_shape=(
            jax.ShapeDtypeStruct((3, 1024, 256), BF16),
            jax.ShapeDtypeStruct((3, 1024, 256), BF16),
            jax.ShapeDtypeStruct((9, 256, 256), BF16),
            jax.ShapeDtypeStruct((9, 256, 256), BF16),
        ),
        in_specs=[pl.BlockSpec(memory_space=pl.ANY)] * 4 + [vmem] * 2 + [pl.BlockSpec(memory_space=pltpu.SMEM)] * 2,
        out_specs=(pl.BlockSpec(memory_space=pl.ANY),) * 4,
        scratch_shapes=[
            pltpu.VMEM((3, 32, 32, 256), BF16),
            pltpu.VMEM((3, 32, 32, 256), BF16),
            pltpu.VMEM((3, 3, 256, 256), BF16),
            pltpu.VMEM((3, 3, 256, 256), BF16),
            pltpu.VMEM((3, 1024, 256), BF16),
            pltpu.VMEM((3, 1024, 256), BF16),
            pltpu.VMEM((9, 256, 256), BF16),
            pltpu.VMEM((9, 256, 256), BF16),
            pltpu.VMEM((3, 1088, 768), BF16),
            pltpu.VMEM((3, 1088, 768), BF16),
            pltpu.VMEM((3, 1088, 768), BF16),
            pltpu.VMEM((3, 768, 256), BF16),
            pltpu.VMEM((3, 1024, 256), F32),
            pltpu.VMEM((3, 1024, 256), F32),
            pltpu.VMEM((3, 256, 1024), BF16),
            pltpu.VMEM((2, 4, 4, 9, 16, 128), F32),
            pltpu.VMEM((2, 4, 4, 9, 16, 128), F32),
            pltpu.VMEM((4, 96, 768), BF16),
            pltpu.VMEM((3, 4, 96, 256), BF16),
            pltpu.VMEM((288, 256), BF16),
            pltpu.VMEM((4, 96, 256), F32),
            pltpu.VMEM((2, 288, 96), F32),
            pltpu.VMEM((128, 1024), BF16),
            pltpu.VMEM((4, 2, 12, 32, 128), BF16),
            *[pltpu.VMEM((96, 32, 128), BF16)] * 4,
            pltpu.VMEM((4, 8, 12, 32, 128), BF16),
            *[pltpu.VMEM((2, 4, 12, 32, 128), BF16)] * 4,
            pltpu.VMEM((2, 1, 128), jnp.int32),
            pltpu.VMEM((2, 8, 128), jnp.int32),
            pltpu.VMEM((8, 1, 128), jnp.int32),
            pltpu.SMEM((8, 1, 128), jnp.int32),
            pltpu.VMEM((6, 4, 4, 3, 16, 128), BF16),
            pltpu.VMEM((6, 4, 4, 3, 16, 128), BF16),
            pltpu.VMEM((6, 4, 4, 3, 16, 128), BF16),
            pltpu.VMEM((6, 4, 4, 3, 16, 128), BF16),
            pltpu.VMEM((6, 4, 3, 16, 128), BF16),
            pltpu.VMEM((6, 4, 3, 16, 128), BF16),
            pltpu.VMEM((6, 3, 16, 128), F32),
            pltpu.VMEM((6, 4, 3, 16, 128), F32),
            pltpu.VMEM((6, 2, 4, 4, 3, 16, 128), BF16),
            dma((7,)),
            dma((8,)),
            dma((4, 7)),
            dma((4, 8)),
            dma((4, 7)),
            dma((4, 8)),
            dma((6, 22)),
            dma((6, 22)),
            dma((4,)),
            dma((4,)),
            dma((4,)),
        ],
        compiler_params=pltpu.CompilerParams(
            collective_id=0, has_side_effects=True, vmem_limit_bytes=67043328
        ),
    )(features[0], cotangent[0], conv_one, conv_two, neighbour_tile, rotation, neighbour_tile, rotation)

    anywhere = pl.BlockSpec(memory_space=pl.ANY)
    out, gfeat, grad1, grad2 = pl.pallas_call(
        functools.partial(results, factor),
        in_specs=[anywhere] * 4,
        out_specs=(anywhere,) * 4,
        out_shape=(
            jax.ShapeDtypeStruct((3072, 256), BF16),
            jax.ShapeDtypeStruct((3072, 256), BF16),
            jax.ShapeDtypeStruct((2304, 256), F32),
            jax.ShapeDtypeStruct((2304, 256), F32),
        ),
        scratch_shapes=[
            pltpu.VMEM((2, 2304, 256), BF16),
            pltpu.VMEM((2, 3072, 256), BF16),
            pltpu.VMEM((2, 2304, 256), F32),
            dma((10,)),
            dma((10,)),
        ],
    )(out.reshape(3072, 256), gfeat.reshape(3072, 256), gout1.reshape(2304, 256), gout2.reshape(2304, 256))
    shape = features.shape
    kshape = conv_one.shape
    return (out.reshape(shape), gfeat.reshape(shape), grad1.reshape(kshape), grad2.reshape(kshape))


def solution(mesh):
    placed = (
        P("members", "tiles", None, None, None),
        P(),
        P(),
        P("members", "tiles", None, None, None),
        P("tiles", None),
        P("tiles", None),
    )
    return jax.shard_map(
        on_device,
        mesh=mesh,
        in_specs=placed,
        out_specs=(
            P("members", "tiles", None, None, None),
            P("members", "tiles", None, None, None),
            P(),
            P(),
        ),
        check_vma=False,
    )
```

```python
import functools
import math

import jax
import jax.numpy as jnp
from jax import lax
from jax.experimental import pallas as pl
from jax.experimental.pallas import tpu as pltpu
from jax.sharding import PartitionSpec as P

MESH = pl.DeviceIdType.MESH
F32 = jnp.float32
BF16 = jnp.bfloat16
ROWS = 1024


ORDER = ("xyz", "yzx", "zxy")


def kernel(
    feat_hbm, cot_hbm, w1_hbm, w2_hbm, near_v, turn_v, near, turn,
    out_hbm, gfeat_hbm, gout1_hbm, gout2_hbm,
    feat, cot, w1, w2, out, gfeat, gout1, gout2,
    fa3, c3, d3, wt, pre, dact, xt, grad1, grad2, seams, edges, rimrows, corr, mats, pickrow,
    edge_out, ag0, ag1, ag2, ag3, pick, got0, got1, got2, got3, tab, tabw, tabv, tabs,
    snd, rcore, sx, rx, sy, ry, sz, rz, full,
    tab_s, tab_r, ag_s, ag_r, pk_s, pk_r, ar_s, ar_r, loc_sem, in_sem, out_sem,
):
    ag = (ag0, ag1, ag2, ag3)
    got = (got0, got1, got2, got3)
    grads = (grad1, grad2)
    gouts = (gout1, gout2)
    loads = [
        pltpu.make_async_copy(src, dst, in_sem.at[i])
        for i, (src, dst) in enumerate(((feat_hbm, feat), (cot_hbm, cot), (w2_hbm, w2), (w1_hbm, w1)))
    ]
    for copy in loads:
        copy.start()
    stores = [
        pltpu.make_async_copy(src, dst, out_sem.at[i])
        for i, (src, dst) in enumerate(((out, out_hbm), (gfeat, gfeat_hbm), (gout1, gout1_hbm), (gout2, gout2_hbm)))
    ]
    me = lax.axis_index("tiles")
    xpos = lax.axis_index("members")
    core = lax.rem(me, 2)
    ypos = lax.rem(me // 2, 4)
    zpos = me // 8
    pos = {"x": xpos, "y": ypos, "z": zpos}
    ring = zpos * (1 - core) + ypos * core
    other = ypos * (1 - core) + zpos * core

    def tid(z, y, c):
        return (z * 4 + y) * 2 + c

    partner = tid(zpos, ypos, 1 - core)

    def wrap(v):
        return lax.rem(v, 4)

    barrier = pltpu.get_barrier_semaphore()
    pl.semaphore_signal(barrier, inc=1, device_id={"tiles": partner}, device_id_type=MESH)
    for d in range(1, 4):
        for c in range(2):
            pl.semaphore_signal(barrier, inc=1, device_id={"tiles": tid(wrap(zpos + d), ypos, c)}, device_id_type=MESH)
            pl.semaphore_signal(barrier, inc=1, device_id={"tiles": tid(zpos, wrap(ypos + d), c)}, device_id_type=MESH)
        pl.semaphore_signal(barrier, inc=1, device_id={"members": wrap(xpos + d)}, device_id_type=MESH)

    r_i = lax.broadcasted_iota(jnp.int32, (128, 1024), 0)
    c_i = lax.broadcasted_iota(jnp.int32, (128, 1024), 1)
    e_i = r_i // 32
    k_i = r_i - e_i * 32
    want = jnp.where(e_i == 0, k_i, jnp.where(e_i == 1, 992 + k_i, jnp.where(e_i == 2, 32 * k_i, 32 * k_i + 31)))
    pickrow[...] = jnp.where(c_i == want, 1.0, 0.0).astype(BF16)
    m_r = lax.broadcasted_iota(jnp.int32, (288, 96), 0)
    m_c = lax.broadcasted_iota(jnp.int32, (288, 96), 1)
    m_b = m_r // 96
    m_t = (m_r - m_b * 96) // 32
    m_j = m_r - m_b * 96 - m_t * 32 + m_b - 1
    inside = (m_j >= 0) & (m_j < 32)
    mats[0] = jnp.where(inside & (m_c == m_t * 32 + m_j), 1.0, 0.0)
    mats[1] = jnp.where(inside & (m_c == m_t * 32 + 31 - m_j), 1.0, 0.0)
    tile_of = m_t

    def remote(src, dst, ssem, rsem, target):
        return pltpu.make_async_remote_copy(
            src_ref=src, dst_ref=dst, send_sem=ssem, recv_sem=rsem,
            device_id={"tiles": target}, device_id_type=MESH,
        )

    def remote_x(src, dst, ssem, rsem, target):
        return pltpu.make_async_remote_copy(
            src_ref=src, dst_ref=dst, send_sem=ssem, recv_sem=rsem,
            device_id={"members": target}, device_id_type=MESH,
        )

    sends = []

    def launch(make):
        make().start()
        sends.append(make)

    def fill_tables():
        way = turn_v[...]
        src = 4 * near_v[...] + (way & 3)
        device = (src * 43691) >> 19
        z_of, y_of, c_of = device >> 3, (device >> 1) & 3, device & 1
        row = src - 12 * device
        for h, at in enumerate((z_of, y_of)):
            tabw[h] = jnp.zeros((8, 128), jnp.int32)
            tabw[h, 0:3, 0:4] = (at * 2 + c_of) * 12 + row
            wide = tabw[h]
            tab[h] = wide[0:1] + pltpu.roll(wide, 4, 1)[1:2] + pltpu.roll(wide, 8, 1)[2:3]

    def dot(a, b):
        return jnp.dot(a, b, preferred_element_type=F32)

    def dot_nt(a, b):
        return lax.dot_general(a, b, (((1,), (1,)), ((), ())), preferred_element_type=F32)

    def dot_tn(a, b):
        return lax.dot_general(a, b, (((0,), (0,)), ((), ())), preferred_element_type=F32)

    def take_edges(get, which):
        for t in range(3):
            picked = dot(pickrow[...], get(t)).astype(BF16)
            for e in range(4):
                edges[which, e, t * 32:t * 32 + 32, :] = picked[e * 32:e * 32 + 32]

    def put_edge(n, t, e, value):
        edge_out[n, 0, t * 4 + e] = value[:, 0:128]
        edge_out[n, 1, t * 4 + e] = value[:, 128:256]

    def put_edges(n, which):
        for t in range(3):
            for e in range(4):
                put_edge(n, t, e, edges[which, e, t * 32:t * 32 + 32, :])

    def send_edges(n):
        for d in range(1, 4):
            launch(lambda d=d: remote(edge_out.at[n, 0], ag[n].at[pl.ds((zpos * 2 + core) * 12, 12)], ag_s.at[n, d - 1], ag_r.at[n, zpos * 2 + core], tid(wrap(zpos + d), ypos, 0)))
            launch(lambda d=d: remote(edge_out.at[n, 1], ag[n].at[pl.ds((ypos * 2 + core) * 12, 12)], ag_s.at[n, d + 2], ag_r.at[n, ypos * 2 + core], tid(zpos, wrap(ypos + d), 1)))
        slot = (zpos * core + ypos * (1 - core)) * 2 + core
        launch(lambda: remote(edge_out.at[n, 1 - core], ag[n].at[pl.ds(slot * 12, 12)], ag_s.at[n, 6], ag_r.at[n, slot], partner))
        own = pltpu.make_async_copy(edge_out.at[n, core], ag[n].at[pl.ds((ring * 2 + core) * 12, 12)], loc_sem.at[1])
        own.start()
        own.wait()

    def forward(n):
        def wait(slot):
            remote(edge_out.at[n, 0], ag[n].at[pl.ds(slot * 12, 12)], ag_s.at[n, 0], ag_r.at[n, slot], partner).wait_recv()

        for d in range(1, 4):
            for c in range(2):
                wait(wrap(ring + d) * 2 + c)
        wait(ring * 2 + 1 - core)

        def choose(q, carry):
            for k in range(12):
                pick[n, q, k] = ag[n][tabs[q, 0, k]]
            return carry

        lax.fori_loop(0, 8, choose, 0)

        def one(d, c):
            p = wrap(other + d)
            target = tid(zpos * (1 - core) + p * core, p * (1 - core) + ypos * core, c)
            return remote(pick.at[n, p * 2 + c], got[n].at[core, other], pk_s.at[n, d * 2 + c - 2], pk_r.at[n, core * 4 + other], target)

        for d in range(1, 4):
            for c in range(2):
                launch(lambda d=d, c=c: one(d, c))
        launch(lambda: remote(pick.at[n, other * 2 + 1 - core], got[n].at[core, other], pk_s.at[n, 6], pk_r.at[n, core * 4 + other], partner))
        own = pltpu.make_async_copy(pick.at[n, other * 2 + core], got[n].at[core, other], loc_sem.at[2])
        own.start()
        own.wait()

    def arrive(n):
        def wait(h, p):
            remote(pick.at[n, 0], got[n].at[h, p], pk_s.at[n, 0], pk_r.at[n, h * 4 + p], partner).wait_recv()

        for d in range(1, 4):
            wait(0, wrap(ypos + d))
            wait(1, wrap(zpos + d))
        wait(1 - core, zpos * (1 - core) + ypos * core)

    def source(k):
        way = turn[k // 4, k % 4]
        device = lax.div(4 * near[k // 4, k % 4] + lax.rem(way, 4), 12)
        return lax.rem(lax.div(device, 2), 4), lax.div(device, 8), lax.div(way, 4)

    def received(n, e):
        rows = []
        for t in range(3):
            k = t * 4 + e
            y_from, z_from, _ = source(k)
            rows.append(jnp.concatenate([got[n][0, y_from, k], got[n][1, z_from, k]], axis=1))
        return jnp.concatenate(rows, axis=0)

    def turned(e, low, high):
        flip = jnp.where(tile_of == 0, source(e)[2], jnp.where(tile_of == 1, source(4 + e)[2], source(8 + e)[2]))[low:high]
        return jnp.where(flip == 1, mats[1, low:high], mats[0, low:high]).astype(BF16)

    def take_seams(n):
        for e in range(4):
            both = dot(turned(e, 0, 288), received(n, e)).astype(BF16)
            for b in range(3):
                seams[e, :, b * 256:b * 256 + 256] = both[b * 96:b * 96 + 96]

    jj = lax.rem(lax.broadcasted_iota(jnp.int32, (128, 256), 0), 32)

    def put3(dst, t, r, x):
        row = pl.multiple_of(32 + r * 128, 32)
        dst[t, pl.ds(row, 128), 256:512] = x.astype(BF16)
        dst[t, pl.ds(row, 128), 0:256] = jnp.where(jj == 0, 0.0, pltpu.roll(x, 1, 0)).astype(BF16)
        dst[t, pl.ds(row, 128), 512:768] = jnp.where(jj == 31, 0.0, pltpu.roll(x, 127, 0)).astype(BF16)

    def each_chunk(body):
        def step(i, carry):
            t = i // 8
            body(t, i - t * 8)
            return carry

        lax.fori_loop(0, 24, step, 0)

    def conv3(x3, weight, store, after=()):
        parts = 1024 // ROWS

        def step(i, carry):
            t = i // parts
            r = (i - t * parts) * ROWS
            acc = dot(x3[t, pl.ds(pl.multiple_of(r, 32), ROWS), :], weight(0))
            acc = acc + dot(x3[t, pl.ds(pl.multiple_of(r + 32, 32), ROWS), :], weight(1))
            acc = acc + dot(x3[t, pl.ds(pl.multiple_of(r + 64, 32), ROWS), :], weight(2))
            store(t, pl.multiple_of(r, 128), acc)
            for at, do in after:
                pl.when(i == at)(do)
            return carry

        lax.fori_loop(0, 3 * parts, step, 0)

    def edge_weight(w, e):
        return [w[0, 0], w[0, 1], w[0, 2]] if e == 0 else [w[2, 0], w[2, 1], w[2, 2]] if e == 1 else [w[0, 0], w[1, 0], w[2, 0]] if e == 2 else [w[0, 2], w[1, 2], w[2, 2]]

    eight = lax.broadcasted_iota(jnp.int32, (8, 256), 0)

    def add_edges(dst, value_of):
        for t in range(3):
            dst[t, 0:32, :] += value_of[0, t * 32:t * 32 + 32, :]
            dst[t, 992:1024, :] += value_of[1, t * 32:t * 32 + 32, :]

        def step(i, carry):
            for t in range(3):
                row = pl.multiple_of(i * 32, 8)
                line = jnp.broadcast_to(value_of[2, pl.ds(t * 32 + i, 1), :], (8, 256))
                dst[t, pl.ds(row, 8), :] += jnp.where(eight == 0, line, 0.0)
                row = pl.multiple_of(i * 32 + 24, 8)
                line = jnp.broadcast_to(value_of[3, pl.ds(t * 32 + i, 1), :], (8, 256))
                dst[t, pl.ds(row, 8), :] += jnp.where(eight == 7, line, 0.0)
            return carry

        lax.fori_loop(0, 32, step, 0)

    def seam_conv(w, dst):
        for e in range(4):
            ws = edge_weight(w, e)
            corr[e] = dot(seams[e, :, 0:256], ws[0]) + dot(seams[e, :, 256:512], ws[1]) + dot(seams[e, :, 512:768], ws[2])
        add_edges(dst, corr)

    def rim_add(n, dst):
        for e in range(4):
            corr[e] = dot(turned(e, 96, 192), received(n, e))
        add_edges(dst, corr)

    def rims(which, w, n):
        shift = mats[0].astype(BF16)
        for e in range(4):
            ws = edge_weight(w, e)
            rimrows[...] = dot(shift, edges[which, e]).astype(BF16)
            value = dot_nt(rimrows[192:288], ws[0]) + dot_nt(rimrows[96:192], ws[1]) + dot_nt(rimrows[0:96], ws[2])
            value = value.astype(BF16)
            for t in range(3):
                put_edge(n, t, e, value[t * 32:t * 32 + 32])

    def transpose_tiles(x3):
        eye = jnp.where(lax.broadcasted_iota(jnp.int32, (256, 256), 0) == lax.broadcasted_iota(jnp.int32, (256, 256), 1), 1.0, 0.0).astype(BF16)
        for t in range(3):
            xt[t] = dot_nt(eye, x3[t, 32:1056, 256:512]).astype(BF16)

    def turn_weight(w):
        for a in range(3):
            for b in range(3):
                wt[a, b * 256:b * 256 + 256, :] = w[2 - a, 2 - b].T

    def grad_inner(g3, dst, after=()):
        def step(i, carry):
            al = i // 3
            be = i - al * 3
            value = None
            for t in range(3):
                part = dot(xt[t], g3[t, pl.ds(pl.multiple_of(al * 32, 32), 1024), pl.ds(pl.multiple_of(be * 256, 256), 256)])
                value = part if value is None else value + part
            for h in range(2):
                dst[h, :, :, 8 - i] = value[:, h * 128:h * 128 + 128].reshape(4, 4, 16, 128)
            for at, do in after:
                pl.when(i == at)(do)
            return carry

        lax.fori_loop(0, 9, step, 0)

    def grad_seams(which, dst):
        for e in range(4):
            value = dot_tn(seams[e], edges[which, e])
            for b in range(3):
                ab = (b, 6 + b, 3 * b, 3 * b + 2)[e]
                for h in range(2):
                    dst[h, :, :, ab] += value[b * 256:b * 256 + 256, h * 128:h * 128 + 128].reshape(4, 4, 16, 128)

    def along(axis, p, src, dst, ssem, rsem):
        if axis == "x":
            return remote_x(src, dst, ssem, rsem, p)
        return remote(src, dst, ssem, rsem, tid(zpos, p, core) if axis == "y" else tid(p, ypos, core))

    def swap(u, axis, base, src_of, dst_of):
        mine = pos[axis]
        for d in range(1, 4):
            def make(d=d):
                p = wrap(pos[axis] + d)
                return along(axis, p, src_of(p), dst_of(pos[axis]), ar_s.at[u, base + d - 1], ar_r.at[u, base + pos[axis]])

            launch(make)

    def swapped(u, axis, base, src_of, dst_of):
        for d in range(1, 4):
            p = wrap(pos[axis] + d)
            along(axis, p, src_of(p), dst_of(p), ar_s.at[u, base], ar_r.at[u, base + p]).wait_recv()

    def core_args(u):
        return (snd.at[u], rcore.at[u], ar_s.at[u, 0], ar_r.at[u, 0], partner)

    def first_args(u, r):
        return (u, ORDER[r][0], 1, lambda p: sx.at[u, p], lambda p: rx.at[u, p])

    def second_args(u, r):
        return (u, ORDER[r][1], 5, lambda p: sy.at[u, p], lambda p: ry.at[u, p])

    def third_args(u, r):
        return (u, ORDER[r][2], 9, lambda p: sz.at[u], lambda p: rz.at[u, p])

    def back_second_args(u, r):
        return (u, ORDER[r][1], 13, lambda p: full.at[u, core, pos[ORDER[r][0]], pos[ORDER[r][1]]], lambda p: full.at[u, core, pos[ORDER[r][0]], p])

    def back_first_args(u, r):
        return (u, ORDER[r][0], 17, lambda p: full.at[u, core, pos[ORDER[r][0]]], lambda p: full.at[u, core, p])

    def step_core(g):
        for r in range(3):
            u = g * 3 + r
            snd[u] = grads[g][1 - core, :, :, 3 * r:3 * r + 3].astype(BF16)
            launch(lambda u=u: remote(*core_args(u)))

    def step_first(g):
        for r in range(3):
            u = g * 3 + r
            remote(*core_args(u)).wait_recv()
            sx[u] = (grads[g][core, :, :, 3 * r:3 * r + 3] + rcore[u].astype(F32)).astype(BF16)
            swap(*first_args(u, r))

    def step_second(g):
        for r in range(3):
            u = g * 3 + r
            swapped(*first_args(u, r))
            mine = pos[ORDER[r][0]]
            total = grads[g][core, mine, :, 3 * r:3 * r + 3] + rcore[u, mine].astype(F32)
            for d in range(1, 4):
                total = total + rx[u, wrap(mine + d)].astype(F32)
            sy[u] = total.astype(BF16)
            swap(*second_args(u, r))

    def step_third(g):
        for r in range(3):
            u = g * 3 + r
            swapped(*second_args(u, r))
            mine = pos[ORDER[r][1]]
            total = sy[u, mine].astype(F32)
            for d in range(1, 4):
                total = total + ry[u, wrap(mine + d)].astype(F32)
            sz[u] = total
            swap(*third_args(u, r))

    def step_back_second(g):
        for r in range(3):
            u = g * 3 + r
            swapped(*third_args(u, r))
            total = sz[u]
            mine = pos[ORDER[r][2]]
            rz[u, mine] = total
            total = (rz[u, 0] + rz[u, 1]) + (rz[u, 2] + rz[u, 3])
            full[u, core, pos[ORDER[r][0]], pos[ORDER[r][1]]] = total.astype(BF16)
            swap(*back_second_args(u, r))

    def step_back_first(g):
        for r in range(3):
            u = g * 3 + r
            swapped(*back_second_args(u, r))
            swap(*back_first_args(u, r))

    def last_args(u, h):
        return (full.at[u, h], full.at[u, h], ar_s.at[u, 21], ar_r.at[u, 21], partner)

    def step_back_core(g):
        for r in range(3):
            u = g * 3 + r
            swapped(*back_first_args(u, r))
            launch(lambda u=u: remote(*last_args(u, core)))

    def step_end(g):
        for r in range(3):
            u = g * 3 + r
            remote(*last_args(u, 1 - core)).wait_recv()
            for b in range(3):
                for h in range(2):
                    gouts[g][3 * r + b, :, h * 128:h * 128 + 128] = full[u, h, :, :, b].reshape(256, 128)

    fill_tables()
    loads[0].wait()
    take_edges(lambda t: feat[t].reshape(1024, 256), 0)
    put_edges(0, 0)
    pl.semaphore_wait(barrier, 16)
    send_edges(0)

    for d in range(1, 4):
        launch(lambda d=d: remote(tab.at[0], tabv.at[ypos * 2 + core], tab_s.at[d - 1], tab_r.at[ypos * 2 + core], tid(zpos, wrap(ypos + d), 0)))
        launch(lambda d=d: remote(tab.at[1], tabv.at[zpos * 2 + core], tab_s.at[d + 2], tab_r.at[zpos * 2 + core], tid(wrap(zpos + d), ypos, 1)))
    slot_p = (ypos * core + zpos * (1 - core)) * 2 + core
    launch(lambda: remote(tab.at[1 - core], tabv.at[slot_p], tab_s.at[6], tab_r.at[slot_p], partner))
    tab_own = pltpu.make_async_copy(tab.at[core], tabv.at[other * 2 + core], loc_sem.at[0])
    tab_own.start()

    loads[1].wait()
    loads[2].wait()
    take_edges(lambda t: cot[t].reshape(1024, 256), 1)
    rims(1, w2, 1)
    send_edges(1)

    for x3 in (fa3, c3, d3):
        x3[:, 0:32, :] = jnp.zeros((3, 32, 768), BF16)
        x3[:, 1056:1088, :] = jnp.zeros((3, 32, 768), BF16)

    def load_feat(t, r):
        put3(fa3, t, r, feat[t, pl.ds(r * 4, 4)].reshape(128, 256).astype(F32))

    def load_cot(t, r):
        put3(c3, t, r, cot[t, pl.ds(r * 4, 4)].reshape(128, 256).astype(F32))

    each_chunk(load_feat)
    for d in range(1, 4):
        for c in range(2):
            slot = wrap(other + d) * 2 + c
            remote(tab.at[0], tabv.at[slot], tab_s.at[0], tab_r.at[slot], partner).wait_recv()
    slot = other * 2 + 1 - core
    remote(tab.at[0], tabv.at[slot], tab_s.at[0], tab_r.at[slot], partner).wait_recv()
    tab_own.wait()
    to_smem = pltpu.make_async_copy(tabv, tabs, loc_sem.at[3])
    to_smem.start()
    to_smem.wait()

    def store_pre(t, r, acc):
        pre[t, pl.ds(r, ROWS), :] = acc

    def store_dact(t, r, acc):
        dact[t, pl.ds(r, ROWS), :] = acc

    loads[3].wait()
    conv3(fa3, lambda a: w1[a].reshape(768, 256), store_pre, ((2, lambda: forward(0)),))
    each_chunk(load_cot)
    turn_weight(w2)
    conv3(c3, lambda a: wt[a], store_dact, ((0, lambda: forward(1)),))
    transpose_tiles(fa3)
    turn_weight(w1)
    arrive(0)
    take_seams(0)
    seam_conv(w1, pre)

    def activate(t, r):
        row = pl.multiple_of(r * 128, 128)
        u = pre[t, pl.ds(row, 128), :]
        s = 1.0 / (1.0 + jnp.exp(-u))
        put3(fa3, t, r, (u * s).astype(BF16).astype(F32))
        pre[t, pl.ds(row, 128), :] = s * (1.0 + u * (1.0 - s))

    each_chunk(activate)

    take_edges(lambda t: fa3[t, 32:1056, 256:512], 2)
    put_edges(2, 2)
    send_edges(2)
    arrive(1)
    rim_add(1, dact)

    def slope(t, r):
        row = pl.multiple_of(r * 128, 128)
        d = dact[t, pl.ds(row, 128), :] * pre[t, pl.ds(row, 128), :]
        put3(d3, t, r, d.astype(BF16).astype(F32))

    each_chunk(slope)
    take_edges(lambda t: d3[t, 32:1056, 256:512], 0)
    rims(0, w1, 3)
    send_edges(3)
    grad_inner(d3, grad1, ((3, lambda: forward(2)),))
    grad_seams(0, grad1)
    step_core(0)
    transpose_tiles(fa3)
    grad_inner(c3, grad2, ((1, lambda: step_first(0)), (3, lambda: forward(3))))
    arrive(2)
    take_seams(2)
    grad_seams(1, grad2)
    step_core(1)
    step_second(0)
    conv3(
        fa3, lambda a: w2[a].reshape(768, 256), store_pre,
        ((0, lambda: step_first(1)), (1, lambda: step_third(0)), (2, lambda: step_second(1))),
    )

    def finish_out(t, r):
        row = pl.multiple_of(r * 128, 128)
        out[t, pl.ds(row, 128), :] = pre[t, pl.ds(row, 128), :].astype(BF16)

    def finish_gfeat(t, r):
        row = pl.multiple_of(r * 128, 128)
        gfeat[t, pl.ds(row, 128), :] = dact[t, pl.ds(row, 128), :].astype(BF16)

    seam_conv(w2, pre)
    step_back_second(0)
    each_chunk(finish_out)
    stores[0].start()
    step_third(1)
    conv3(
        d3, lambda a: wt[a], store_dact,
        ((0, lambda: step_back_first(0)), (1, lambda: step_back_second(1))),
    )
    arrive(3)
    rim_add(3, dact)
    step_back_core(0)
    step_back_first(1)
    each_chunk(finish_gfeat)
    stores[1].start()
    step_end(0)
    stores[2].start()
    step_back_core(1)
    step_end(1)
    stores[3].start()
    for copy in stores:
        copy.wait()
    for make in sends:
        make().wait_send()


def results(factor, out_in, gfeat_in, g1_in, g2_in, out, gfeat, g1, g2, held_g, held, total, sem_in, sem_out):
    pieces = [(i, g_in, g, 768 * r) for r in range(3) for i, (g_in, g) in enumerate(((g1_in, g1), (g2_in, g2)))]
    gets = [
        pltpu.make_async_copy(g_in.at[pl.ds(row, 768)], held_g.at[i, pl.ds(row, 768)], sem_in.at[n])
        for n, (i, g_in, g, row) in enumerate(pieces)
    ]
    puts = [
        pltpu.make_async_copy(total.at[i, pl.ds(row, 768)], g.at[pl.ds(row, 768)], sem_out.at[n])
        for n, (i, g_in, g, row) in enumerate(pieces)
    ]
    fields = [(i, f_in, f, 1536 * r) for r in range(2) for i, (f_in, f) in enumerate(((out_in, out), (gfeat_in, gfeat)))]
    gets += [
        pltpu.make_async_copy(f_in.at[pl.ds(row, 1536)], held.at[i, pl.ds(row, 1536)], sem_in.at[6 + n])
        for n, (i, f_in, f, row) in enumerate(fields)
    ]
    puts += [
        pltpu.make_async_copy(held.at[i, pl.ds(row, 1536)], f.at[pl.ds(row, 1536)], sem_out.at[6 + n])
        for n, (i, f_in, f, row) in enumerate(fields)
    ]
    for copy in gets:
        copy.start()
    for n, (i, g_in, g, row) in enumerate(pieces):
        gets[n].wait()
        total[i, pl.ds(row, 768)] = held_g[i, pl.ds(row, 768)].astype(F32) * factor
        puts[n].start()
    for n in range(6, 10):
        gets[n].wait()
        puts[n].start()
    for copy in puts:
        copy.wait()


def on_device(features, conv_one, conv_two, cotangent, neighbour_tile, rotation):
    cells_all = lax.axis_size("members") * lax.axis_size("tiles") * 3 * 1024
    factor = 1.0 / math.sqrt(cells_all)
    vmem = pl.BlockSpec(memory_space=pltpu.VMEM)
    dma = pltpu.SemaphoreType.DMA
    out, gfeat, gout1, gout2 = pl.pallas_call(
        kernel,
        out_shape=(
            jax.ShapeDtypeStruct((3, 1024, 256), BF16),
            jax.ShapeDtypeStruct((3, 1024, 256), BF16),
            jax.ShapeDtypeStruct((9, 256, 256), BF16),
            jax.ShapeDtypeStruct((9, 256, 256), BF16),
        ),
        in_specs=[pl.BlockSpec(memory_space=pl.ANY)] * 4 + [vmem] * 2 + [pl.BlockSpec(memory_space=pltpu.SMEM)] * 2,
        out_specs=(pl.BlockSpec(memory_space=pl.ANY),) * 4,
        scratch_shapes=[
            pltpu.VMEM((3, 32, 32, 256), BF16),
            pltpu.VMEM((3, 32, 32, 256), BF16),
            pltpu.VMEM((3, 3, 256, 256), BF16),
            pltpu.VMEM((3, 3, 256, 256), BF16),
            pltpu.VMEM((3, 1024, 256), BF16),
            pltpu.VMEM((3, 1024, 256), BF16),
            pltpu.VMEM((9, 256, 256), BF16),
            pltpu.VMEM((9, 256, 256), BF16),
            pltpu.VMEM((3, 1088, 768), BF16),
            pltpu.VMEM((3, 1088, 768), BF16),
            pltpu.VMEM((3, 1088, 768), BF16),
            pltpu.VMEM((3, 768, 256), BF16),
            pltpu.VMEM((3, 1024, 256), F32),
            pltpu.VMEM((3, 1024, 256), F32),
            pltpu.VMEM((3, 256, 1024), BF16),
            pltpu.VMEM((2, 4, 4, 9, 16, 128), F32),
            pltpu.VMEM((2, 4, 4, 9, 16, 128), F32),
            pltpu.VMEM((4, 96, 768), BF16),
            pltpu.VMEM((3, 4, 96, 256), BF16),
            pltpu.VMEM((288, 256), BF16),
            pltpu.VMEM((4, 96, 256), F32),
            pltpu.VMEM((2, 288, 96), F32),
            pltpu.VMEM((128, 1024), BF16),
            pltpu.VMEM((4, 2, 12, 32, 128), BF16),
            *[pltpu.VMEM((96, 32, 128), BF16)] * 4,
            pltpu.VMEM((4, 8, 12, 32, 128), BF16),
            *[pltpu.VMEM((2, 4, 12, 32, 128), BF16)] * 4,
            pltpu.VMEM((2, 1, 128), jnp.int32),
            pltpu.VMEM((2, 8, 128), jnp.int32),
            pltpu.VMEM((8, 1, 128), jnp.int32),
            pltpu.SMEM((8, 1, 128), jnp.int32),
            pltpu.VMEM((6, 4, 4, 3, 16, 128), BF16),
            pltpu.VMEM((6, 4, 4, 3, 16, 128), BF16),
            pltpu.VMEM((6, 4, 4, 3, 16, 128), BF16),
            pltpu.VMEM((6, 4, 4, 3, 16, 128), BF16),
            pltpu.VMEM((6, 4, 3, 16, 128), BF16),
            pltpu.VMEM((6, 4, 3, 16, 128), BF16),
            pltpu.VMEM((6, 3, 16, 128), F32),
            pltpu.VMEM((6, 4, 3, 16, 128), F32),
            pltpu.VMEM((6, 2, 4, 4, 3, 16, 128), BF16),
            dma((7,)),
            dma((8,)),
            dma((4, 7)),
            dma((4, 8)),
            dma((4, 7)),
            dma((4, 8)),
            dma((6, 22)),
            dma((6, 22)),
            dma((4,)),
            dma((4,)),
            dma((4,)),
        ],
        compiler_params=pltpu.CompilerParams(
            collective_id=0, has_side_effects=True, vmem_limit_bytes=67043328
        ),
    )(features[0], cotangent[0], conv_one, conv_two, neighbour_tile, rotation, neighbour_tile, rotation)

    anywhere = pl.BlockSpec(memory_space=pl.ANY)
    out, gfeat, grad1, grad2 = pl.pallas_call(
        functools.partial(results, factor),
        in_specs=[anywhere] * 4,
        out_specs=(anywhere,) * 4,
        out_shape=(
            jax.ShapeDtypeStruct((3072, 256), BF16),
            jax.ShapeDtypeStruct((3072, 256), BF16),
            jax.ShapeDtypeStruct((2304, 256), F32),
            jax.ShapeDtypeStruct((2304, 256), F32),
        ),
        scratch_shapes=[
            pltpu.VMEM((2, 2304, 256), BF16),
            pltpu.VMEM((2, 3072, 256), BF16),
            pltpu.VMEM((2, 2304, 256), F32),
            dma((10,)),
            dma((10,)),
        ],
    )(out.reshape(3072, 256), gfeat.reshape(3072, 256), gout1.reshape(2304, 256), gout2.reshape(2304, 256))
    shape = features.shape
    kshape = conv_one.shape
    return (out.reshape(shape), gfeat.reshape(shape), grad1.reshape(kshape), grad2.reshape(kshape))


def solution(mesh):
    placed = (
        P("members", "tiles", None, None, None),
        P(),
        P(),
        P("members", "tiles", None, None, None),
        P("tiles", None),
        P("tiles", None),
    )
    return jax.shard_map(
        on_device,
        mesh=mesh,
        in_specs=placed,
        out_specs=(
            P("members", "tiles", None, None, None),
            P("members", "tiles", None, None, None),
            P(),
            P(),
        ),
        check_vma=False,
    )
```
